32 devices in a mesh: tm: 4 (over z), sx: 4 (over y, x), sy: 2 (over core).
Axes of the slice: x: 2, y: 2, z: 4, core: 2. Of those that a mesh axis runs over, the one named last changes fastest.
Arguments:
- state_guess: float32 [4, 2, 256, 512], P('tm', None, 'sx', 'sy'), may hold values from -6 to 6
- adjoint_guess: float32 [4, 2, 256, 512], P('tm', None, 'sx', 'sy'), may hold values from -6 to 6
- diffusivity: float32 [256, 512], P('sx', 'sy'), may hold values from 0.25 to 2
- decay_rate: float32 [256, 512], P('sx', 'sy'), may hold values from 0.003 to 0.1
- coupling: float32 [256, 512], P('sx', 'sy'), may hold values from -0.7 to 0.7
- control: float32 [2, 256, 512], P(None, 'sx', 'sy'), may hold values from -6 to 6
- target: float32 [2, 256, 512], P(None, 'sx', 'sy'), may hold values from -6 to 6
Outputs:
- state_points: float32 [4, 2, 256, 512], P('tm', None, 'sx', 'sy')
- adjoint_points: float32 [4, 2, 256, 512], P('tm', None, 'sx', 'sy')
- gradient: float32 [256, 512], P('sx', 'sy')
The draws below stay inside these ranges and needn't reach their ends.
All inputs are finite; a program needn't handle non-finite values.
Results may differ from the reference program's by a relative error of at most 0.00002.
Values sent between devices are 32-bit elements; how exact they have to be, the bound alone decides.
No kernel may reach another device: no remote copies, remote signals or barrier semaphores. Data moves between devices by JAX's collectives and lax.ppermute only.
A program may use at most 128 MiB of HBM per device.

```python
import math
import jax
import jax.numpy as jnp
from jax import lax

STEPS = 8
SLABS = 4
NX = 256
NY = 512


def steps_of(stream_key, dims, shards, low, largest):
    def one(axis_at, shards_of):
        heights = jax.random.uniform(jax.random.fold_in(jax.random.fold_in(stream_key, 6), axis_at), (shards_of,), jnp.float32, low / len(shards), largest / len(shards))
        return jnp.repeat(jnp.exp(heights), dims[axis_at] // shards_of).reshape((-1,) + (1,) * (len(dims) - axis_at - 1))

    loudness = one(*shards[0])
    for cut in shards[1:]:
        loudness = loudness * one(*cut)
    return loudness


def centred(own_key, extent, spread, limit, cuts=(), dtype=jnp.bfloat16):
    values = spread * jax.random.normal(own_key, extent, jnp.float32)
    if cuts:
        values = values * steps_of(own_key, extent, cuts, -0.22, 0.18)
    return jnp.clip(values, -limit, limit).astype(dtype)


def setup_inputs(seed: int = 0) -> dict:
    splits = jax.random.split(jax.random.key(seed), 8)
    state_guess = centred(splits[0], (SLABS, 2, NX, NY), 1.0, 6.0, ((0, 4), (2, 4), (3, 2)), jnp.float32)
    adjoint_guess = centred(splits[1], (SLABS, 2, NX, NY), 1.0, 6.0, ((0, 4), (2, 4), (3, 2)), jnp.float32)
    diffusivity = jnp.clip(jnp.exp(math.log(2.0) - 2.0794415 * jax.random.uniform(splits[2], (NX, NY), jnp.float32) ** steps_of(splits[2], (NX, NY), ((0, 4), (1, 2)), -0.2, 0.2)), 0.25, 2.0)
    decay_rate = jnp.clip(jnp.exp(math.log(0.1) - 3.506558 * jax.random.uniform(splits[3], (NX, NY), jnp.float32) ** steps_of(splits[3], (NX, NY), ((0, 4), (1, 2)), -0.2, 0.2)), 0.003, 0.1)
    coupling = jnp.clip(jax.random.uniform(splits[4], (NX, NY), jnp.float32, -0.7, 0.7) * steps_of(splits[4], (NX, NY), ((0, 4), (1, 2)), -0.4, 0.0), -0.7, 0.7)
    control = centred(splits[5], (2, NX, NY), 1.0, 6.0, ((1, 4), (2, 2)), jnp.float32)
    target = centred(splits[6], (2, NX, NY), 1.0, 6.0, ((1, 4), (2, 2)), jnp.float32)
    return {"state_guess": state_guess, "adjoint_guess": adjoint_guess, "diffusivity": diffusivity, "decay_rate": decay_rate, "coupling": coupling, "control": control, "target": target}


TIME_STEP = 0.1
DIFFUSION_FIRST = 1.0
DIFFUSION_SECOND = 0.4
NEIGHBOURS = ((0, 1), (2, 1), (1, 0), (1, 2))


def pad_grid(field):
    return jnp.pad(field, [(0, 0)] * (field.ndim - 2) + [(1, 1), (1, 1)])


def stepped(padded, kappa_pad, decay_rate, coupling, source):
    height = padded.shape[-2] - 2
    width = padded.shape[-1] - 2
    centre = padded[..., 1:-1, 1:-1]
    kappa_mid = kappa_pad[1:-1, 1:-1]
    summed = jnp.zeros(centre.shape, jnp.float32)
    for a, b in NEIGHBOURS:
        summed = summed + 0.5 * (kappa_mid + kappa_pad[a:a + height, b:b + width]) * (padded[..., a:a + height, b:b + width] - centre)
    first = centre[..., 0, :, :]
    second = centre[..., 1, :, :]
    new_first = first + TIME_STEP * (DIFFUSION_FIRST * summed[..., 0, :, :] + decay_rate * (coupling * second - first))
    new_second = second + TIME_STEP * (DIFFUSION_SECOND * summed[..., 1, :, :] + decay_rate * (coupling * first - 2.0 * second))
    result = jnp.stack([new_first, new_second], axis=-3)
    if source is not None:
        result = result + TIME_STEP * source
    return result


def face_product(state_pad, adjoint_pad):
    height = state_pad.shape[-2] - 2
    width = state_pad.shape[-1] - 2
    state_mid = state_pad[..., 1:-1, 1:-1]
    adjoint_mid = adjoint_pad[..., 1:-1, 1:-1]
    summed = jnp.zeros(state_mid.shape, jnp.float32)
    for a, b in NEIGHBOURS:
        summed = summed + (state_pad[..., a:a + height, b:b + width] - state_mid) * (adjoint_mid - adjoint_pad[..., a:a + height, b:b + width])
    return TIME_STEP * 0.5 * (DIFFUSION_FIRST * summed[..., 0, :, :] + DIFFUSION_SECOND * summed[..., 1, :, :])


def reference(state_guess, adjoint_guess, diffusivity, decay_rate, coupling, control, target):
    kappa_pad = pad_grid(diffusivity)

    def sweep(field, source):
        for k in range(STEPS):
            field = stepped(pad_grid(field), kappa_pad, decay_rate, coupling, source)
        return field

    factor = STEPS * TIME_STEP * decay_rate
    g_diag_one = 1.0 - factor
    g_side = factor * coupling
    g_diag_two = 1.0 - 2.0 * factor

    def coarse_step(carry, residual):
        moved = jnp.stack([g_diag_one * carry[0] + g_side * carry[1], g_side * carry[0] + g_diag_two * carry[1]])
        fresh = moved + residual
        return fresh, fresh

    ends = sweep(state_guess, control)
    state_residual = jnp.concatenate([-state_guess[:1], ends[:-1] - state_guess[1:]], axis=0)
    _, state_error = lax.scan(coarse_step, jnp.zeros((2, NX, NY), jnp.float32), state_residual)
    state_points = state_guess + state_error
    final = sweep(state_points[-1], control)
    backs = sweep(adjoint_guess, None)
    last_residual = (final - target - adjoint_guess[-1])[None]
    adjoint_residual = jnp.concatenate([backs[1:] - adjoint_guess[:-1], last_residual], axis=0)
    _, adjoint_error = lax.scan(coarse_step, jnp.zeros((2, NX, NY), jnp.float32), adjoint_residual, reverse=True)
    adjoint_points = adjoint_guess + adjoint_error

    def slab_gradient(summed, pair):
        state_start, adjoint_start = pair
        history = []
        field = state_start
        for k in range(STEPS):
            padded = pad_grid(field)
            history.append(padded)
            field = stepped(padded, kappa_pad, decay_rate, coupling, control)
        adjoint = adjoint_start
        for k in range(STEPS):
            padded = pad_grid(adjoint)
            summed = summed + face_product(history[STEPS - 1 - k], padded)
            adjoint = stepped(padded, kappa_pad, decay_rate, coupling, None)
        return summed, 0.0

    gradient, _ = lax.scan(slab_gradient, jnp.zeros((NX, NY), jnp.float32), (state_points, adjoint_points))
    return state_points, adjoint_points, gradient
```

```python
import functools

import jax
import jax.numpy as jnp
from jax import lax
from jax.experimental import pallas as pl
from jax.experimental.pallas import tpu as pltpu
from jax.sharding import PartitionSpec as P

STEPS = 8
TIME_STEP = 0.1
DIFFUSION = (1.0, 0.4)
DECAY = (1.0, 2.0)

LANES = 128
SUB = 8
PER_GROUP = 4
HALO = 3 * STEPS
HALO_W = 2 * STEPS
SIDE = 32
BLOCK = 8

VMEM_SPEC = pl.BlockSpec(memory_space=pltpu.VMEM)


def call(body, outs, scratch=(), limit=32 << 20):
    return pl.pallas_call(
        body,
        out_shape=[jax.ShapeDtypeStruct(s, jnp.float32) for s in outs],
        out_specs=[VMEM_SPEC] * len(outs),
        scratch_shapes=list(scratch),
        compiler_params=pltpu.CompilerParams(vmem_limit_bytes=limit),
    )


def strip_body(s_ref, a_ref, k_ref, r_ref, c_ref, q_ref, t_ref, out_ref):
    first = lax.axis_index("sy") == 0
    at = 0
    for ref in (s_ref, a_ref, k_ref, r_ref, c_ref, q_ref, t_ref):
        rows, cols = ref.shape
        out_ref[at : at + rows, :] = jnp.where(
            first, ref[:, cols - LANES :], ref[:, :LANES]
        )
        at += rows


def window_body(count, s_ref, a_ref, k_ref, r_ref, c_ref, q_ref, t_ref, strip_ref, *rest):
    outs, coef_ref, ext = rest[:count], rest[count], rest[count + 1]
    me = lax.axis_index("tm")
    first = lax.axis_index("sy") == 0
    at = 0
    for ref in (s_ref, a_ref, k_ref, r_ref, c_ref, q_ref, t_ref):
        rows, cols = ref.shape
        strip = strip_ref[at : at + rows, :]
        zero = jnp.zeros_like(strip)
        ext[at : at + rows, 0:LANES] = jnp.where(first, zero, strip)
        ext[at : at + rows, LANES : LANES + cols] = ref[...]
        ext[at : at + rows, LANES + cols : 2 * LANES + cols] = jnp.where(first, strip, zero)
        at += rows
    guesses = s_ref.shape[0] + a_ref.shape[0]
    wide = s_ref.shape[1] // count

    def window(lo, hi, t):
        start = LANES - SIDE + wide * t
        base = pl.multiple_of((start // LANES) * LANES, LANES)
        shift = 2 * LANES - start % LANES
        return pltpu.roll(ext[lo:hi, pl.ds(base, 2 * LANES)], shift, 1)[:, :LANES]

    for d in range(count):
        outs[d][...] = window(0, guesses, me ^ d)
    coef_ref[...] = window(guesses, at, me)


def interleave_body(count, tile_rows, *refs):
    cens, coef_ref = refs[:count], refs[count]
    mid_s, mid_a, down_ref, up_ref = refs[count + 1 : count + 5]
    me = lax.axis_index("tm")
    groups = count // PER_GROUP
    for d in range(count):
        slab = me ^ d
        g, j = slab // PER_GROUP, slab % PER_GROUP
        for field, mid in ((0, mid_s), (1, mid_a)):
            for sp in range(2):
                rows = cens[d][(2 * field + sp) * tile_rows : (2 * field + sp + 1) * tile_rows, :]
                mid[g, pl.ds(sp * PER_GROUP + j, tile_rows, stride=SUB), :] = rows
    for ref, low in ((down_ref, False), (up_ref, True)):
        at = 0
        for mid, halo in ((mid_s, HALO), (mid_a, HALO_W)):
            size = halo * SUB
            start = 0 if low else (tile_rows - halo) * SUB
            for g in range(groups):
                ref[at : at + size, :] = mid[g, start : start + size, :]
                at += size
        for f in range(7):
            start = f * tile_rows + (0 if low else tile_rows - HALO)
            ref[at : at + HALO, :] = coef_ref[start : start + HALO, :]
            at += HALO


def main_body(count, tile_rows, wide, mid_s, mid_a, coef_ref, top_ref, bot_ref, *rest):
    outs = rest[:count]
    work, hist, lag, cv, ce, cd, cx, cq, gd, tg, fv, fh, flat = rest[count:]
    groups = count // PER_GROUP
    total = tile_rows + 2 * HALO
    me = lax.axis_index("tm")
    s_at = lax.axis_index("sx")
    has_top = s_at > 0
    has_bot = s_at < lax.axis_size("sx") - 1
    end = HALO + tile_rows

    def each_group(fn):
        if groups == 1:
            fn(0)
        else:
            lax.fori_loop(0, groups, lambda g, c: (fn(g), c)[1], 0)

    def masked(flag, value):
        return jnp.where(flag, value, jnp.zeros_like(value))

    at = groups * (HALO + HALO_W) * SUB
    fields = []
    for f in range(7):
        flat[f, 0:HALO, :] = masked(has_top, top_ref[at + f * HALO : at + (f + 1) * HALO, :])
        flat[f, HALO:end, :] = coef_ref[f * tile_rows : (f + 1) * tile_rows, :]
        flat[f, end:total, :] = masked(has_bot, bot_ref[at + f * HALO : at + (f + 1) * HALO, :])
        fields.append(flat[f])
    k, rate, coupling, q0, q1, t0, t1 = fields
    row = lax.broadcasted_iota(jnp.int32, (total, LANES), 0) + (s_at * tile_rows - HALO)
    col = lax.broadcasted_iota(jnp.int32, (total, LANES), 1) + (
        lax.axis_index("sy") * (wide * count) + me * wide - SIDE
    )
    all_rows = tile_rows * lax.axis_size("sx")
    all_cols = wide * count * lax.axis_size("sy")
    half = 0.5 * TIME_STEP
    above = half * (k + pltpu.roll(k, 1, 0))
    below = half * (k + pltpu.roll(k, total - 1, 0))
    east = half * (k + pltpu.roll(k, LANES - 1, 1))
    west = half * (k + pltpu.roll(k, 1, 1))
    faces = above + below + east + west
    above = jnp.where((row >= 1) & (row < all_rows), above, 0.0)
    east = jnp.where((col >= 0) & (col < all_cols - 1), east, 0.0)
    react = TIME_STEP * rate
    cross = react * coupling
    for sp, source in ((0, q0), (1, q1)):
        spread = (
            (cv, DIFFUSION[sp] * above),
            (ce, DIFFUSION[sp] * east),
            (cd, 1.0 - DIFFUSION[sp] * faces - DECAY[sp] * react),
            (cx, cross),
            (cq, TIME_STEP * source),
            (gd, 1.0 - (DECAY[sp] * STEPS) * react),
        )
        for ref, value in spread:
            for j in range(PER_GROUP):
                ref[pl.ds(sp * PER_GROUP + j, total, stride=SUB), :] = value
    tg[pl.ds(PER_GROUP - 1, total, stride=SUB), :] = t0
    tg[pl.ds(SUB - 1, total, stride=SUB), :] = t1

    def blocks(lo, hi):
        return [(r, min(r + BLOCK, hi)) for r in range(lo, hi, BLOCK)]

    def shift(value, by):
        n = value.shape[0] // SUB
        return pltpu.roll(value.reshape(n, SUB, LANES), by, 1).reshape(n * SUB, LANES)

    def at_rows(ref, lo, hi):
        return ref[lo * SUB : hi * SUB, :]

    def step(src, dst, lo, hi, off, source):
        for a, b in blocks(lo, hi):
            u = at_rows(src, a - off, b - off)
            e = at_rows(ce, a, b)
            new = (
                at_rows(cd, a, b) * u
                + at_rows(cv, a, b) * at_rows(src, a - off - 1, b - off - 1)
                + at_rows(cv, a + 1, b + 1) * at_rows(src, a - off + 1, b - off + 1)
                + e * pltpu.roll(u, LANES - 1, 1)
                + pltpu.roll(e * u, 1, 1)
                + at_rows(cx, a, b) * shift(u, PER_GROUP)
            )
            if source:
                new = new + at_rows(cq, a, b)
            dst[(a - off) * SUB : (b - off) * SUB, :] = new

    def sweep(lo, hi, source):
        def turn(t, carry):
            src = jnp.where(t == 0, 0, 1 + (t + 1) % 2)
            dst = 1 + t % 2
            each_group(lambda g: step(work.at[src, g], work.at[dst, g], lo, hi, 0, source))
            return carry

        lax.fori_loop(0, STEPS, turn, 0)
        return 1 + (STEPS - 1) % 2

    def coarse(value, a, b):
        return at_rows(gd, a, b) * value + (STEPS * at_rows(cx, a, b)) * shift(value, PER_GROUP)

    def load(mid, halo, at):
        def one(g):
            size = halo * SUB
            here = at + g * size
            if groups > 1:
                here = pl.multiple_of(here, SUB)
            work[0, g, (HALO - halo) * SUB : HALO * SUB, :] = masked(
                has_top, top_ref[pl.ds(here, size), :]
            )
            work[0, g, HALO * SUB : end * SUB, :] = mid[g]
            work[0, g, end * SUB : (end + halo) * SUB, :] = masked(
                has_bot, bot_ref[pl.ds(here, size), :]
            )

        each_group(one)

    def slab_of(a, b):
        return lax.broadcasted_iota(jnp.int32, ((b - a) * SUB, LANES), 0) % PER_GROUP

    lo, hi = STEPS, total - STEPS
    load(mid_s, HALO, 0)
    last = sweep(1, total - 1, True)
    for a, b in blocks(lo, hi):
        slab = slab_of(a, b)
        carry = jnp.zeros(((b - a) * SUB, LANES), jnp.float32)

        def chain(g, carry, a=a, b=b, slab=slab):
            x = at_rows(work.at[last, g], a, b) - coarse(at_rows(work.at[0, g], a, b), a, b)
            value = carry
            for _ in range(PER_GROUP - 1):
                value = jnp.where(slab == 0, carry, shift(coarse(value, a, b) + x, 1))
            hist[0, g, (a - lo) * SUB : (b - lo) * SUB, :] = value
            return shift(coarse(value, a, b) + x, SUB - PER_GROUP + 1)

        if groups == 1:
            chain(0, carry)
        else:
            lax.fori_loop(0, groups, chain, carry)

    load(mid_a, HALO_W, groups * HALO * SUB)
    last = sweep(STEPS + 1, total - STEPS - 1, False)
    w_lo, w_hi = 2 * STEPS, total - 2 * STEPS

    def keep(g):
        for a, b in blocks(w_lo, w_hi):
            lag[g, (a - w_lo) * SUB : (b - w_lo) * SUB, :] = at_rows(
                work.at[last, g], a, b
            ) - coarse(at_rows(work.at[0, g], a, b), a, b)

    each_group(keep)

    def forward(t, carry):
        each_group(lambda g: step(hist.at[t, g], hist.at[t + 1, g], lo + 1, hi - 1, lo, True))
        return carry

    lax.fori_loop(0, STEPS, forward, 0)

    for a, b in blocks(w_lo, w_hi):
        slab = slab_of(a, b)
        carry = at_rows(hist.at[STEPS, groups - 1], a - lo, b - lo) - at_rows(tg, a, b)

        def unchain(turn, carry, a=a, b=b, slab=slab):
            g = groups - 1 - turn
            y = lag[g, (a - w_lo) * SUB : (b - w_lo) * SUB, :]
            top = jnp.where(slab == PER_GROUP - 1, carry, 0.0)
            value = top
            for _ in range(PER_GROUP - 1):
                value = jnp.where(
                    slab == PER_GROUP - 1, top, shift(coarse(value, a, b) + y, SUB - 1)
                )
            work[0, g, a * SUB : b * SUB, :] = value
            return shift(coarse(value, a, b) + y, PER_GROUP - 1)

        if groups == 1:
            unchain(0, carry)
        else:
            lax.fori_loop(0, groups, unchain, carry)

    lane = lax.broadcasted_iota(jnp.int32, (tile_rows, LANES), 1)
    left = lane < LANES // 2

    def paired(first, second):
        return jnp.where(
            left,
            pltpu.roll(first, LANES - SIDE, 1),
            pltpu.roll(second, LANES // 2 - SIDE, 1),
        )

    for d in range(count):
        slab = me ^ d
        g, j = slab // PER_GROUP, slab % PER_GROUP
        s_rows = [
            hist[0, g, pl.ds((HALO - lo) * SUB + sp * PER_GROUP + j, tile_rows, stride=SUB), :]
            for sp in range(2)
        ]
        w_rows = [
            work[0, g, pl.ds(HALO * SUB + sp * PER_GROUP + j, tile_rows, stride=SUB), :]
            for sp in range(2)
        ]
        outs[d][0:tile_rows, :] = paired(*s_rows)
        outs[d][tile_rows : 2 * tile_rows, :] = paired(*w_rows)

    fv[...] = jnp.zeros_like(fv)
    fh[...] = jnp.zeros_like(fh)

    def products(u, w):
        for a, b in blocks(HALO, end + 1):
            at = slice((a - HALO) * SUB, (b - HALO) * SUB)
            uc, wc = at_rows(u, a - lo, b - lo), at_rows(w, a, b)
            fv[at, :] += (uc - at_rows(u, a - lo - 1, b - lo - 1)) * (
                wc - at_rows(w, a - 1, b - 1)
            )
            if b <= end:
                fh[at, :] += (pltpu.roll(uc, LANES - 1, 1) - uc) * (
                    pltpu.roll(wc, LANES - 1, 1) - wc
                )

    def back(t, carry):
        src = jnp.where(t == 0, 0, 1 + (t + 1) % 2)
        dst = 1 + t % 2

        def one(g):
            products(hist.at[STEPS - 1 - t, g], work.at[src, g])
            step(work.at[src, g], work.at[dst, g], w_lo + 1, w_hi - 1, 0, False)

        each_group(one)
        return carry

    lax.fori_loop(0, STEPS - 1, back, 0)
    last = 1 + (STEPS - 2) % 2
    each_group(lambda g: products(hist.at[0, g], work.at[last, g]))

    size = tile_rows * SUB
    fh[...] = fv[0:size, :] + fv[SUB : size + SUB, :] + fh[...] + pltpu.roll(fh[...], 1, 1)
    summed = []
    for sp in range(2):
        parts = [
            fh[pl.ds(sp * PER_GROUP + j, tile_rows, stride=SUB), :] for j in range(PER_GROUP)
        ]
        summed.append((parts[0] + parts[1]) + (parts[2] + parts[3]))
    gradient = -half * (DIFFUSION[0] * summed[0] + DIFFUSION[1] * summed[1])
    middle = tile_rows // 2
    fold = jnp.where(
        left[:middle],
        pltpu.roll(gradient[:middle], LANES - SIDE, 1),
        pltpu.roll(gradient[middle:], LANES // 2 - SIDE, 1),
    )
    for d in range(count):
        outs[d][2 * tile_rows :, :] = fold


def collect_body(count, wide, *refs):
    parts = refs[:count]
    s_ref, w_ref, g_ref, held = refs[count:]
    me = lax.axis_index("tm")
    for d in range(count):
        held[me ^ d] = parts[d][...]
    rows = g_ref.shape[0]
    middle = rows // 2
    per = LANES // wide
    lane = lax.broadcasted_iota(jnp.int32, (rows, LANES), 1)

    def joined(lo, hi, start, v):
        value = None
        for i in range(per):
            t = v * per + i
            piece = held[t, lo:hi, :]
            turn = (i * wide - start) % LANES
            if turn:
                piece = pltpu.roll(piece, turn, 1)
            value = piece if i == 0 else jnp.where(lane[: hi - lo] >= i * wide, piece, value)
        return value

    for v in range(count // per):
        at = slice(v * LANES, (v + 1) * LANES)
        for sp in range(2):
            start = sp * (LANES // 2)
            s_ref[sp * rows : (sp + 1) * rows, at] = joined(0, rows, start, v)
            w_ref[sp * rows : (sp + 1) * rows, at] = joined(rows, 2 * rows, start, v)
            g_ref[sp * middle : (sp + 1) * middle, at] = joined(
                2 * rows, 2 * rows + middle, start, v
            )


def local(state_guess, adjoint_guess, diffusivity, decay_rate, coupling, control, target):
    rows, cols = diffusivity.shape
    count = lax.axis_size("tm")
    groups = count // PER_GROUP
    wide = cols // count
    total = rows + 2 * HALO
    fields = (
        state_guess.reshape(2 * rows, cols),
        adjoint_guess.reshape(2 * rows, cols),
        diffusivity,
        decay_rate,
        coupling,
        control.reshape(2 * rows, cols),
        target.reshape(2 * rows, cols),
    )

    def swapped(value, d):
        return lax.ppermute(value, "tm", [(i, i ^ d) for i in range(count)])

    def turned(value, d):
        n = lax.axis_size("sx")
        return lax.ppermute(value, "sx", [(i, (i + d) % n) for i in range(n)])

    (strip,) = call(strip_body, [(11 * rows, LANES)])(*fields)
    strip = lax.ppermute(strip, "sy", [(0, 1), (1, 0)])
    *cens, coef = call(
        functools.partial(window_body, count),
        [(4 * rows, LANES)] * count + [(7 * rows, LANES)],
        [pltpu.VMEM((11 * rows, cols + 2 * LANES), jnp.float32)],
    )(*fields, strip)
    cens = [cens[0]] + [swapped(cens[d], d) for d in range(1, count)]
    edge = groups * (HALO + HALO_W) * SUB + 7 * HALO
    mid = (groups, rows * SUB, LANES)
    mid_s, mid_a, down, up = call(
        functools.partial(interleave_body, count, rows),
        [mid, mid, (edge, LANES), (edge, LANES)],
    )(*cens, coef)
    top = turned(down, 1)
    bot = turned(up, -1)
    plain = pltpu.VMEM((total * SUB, LANES), jnp.float32)
    outs = call(
        functools.partial(main_body, count, rows, wide),
        [(2 * rows + rows // 2, LANES)] * count,
        [
            pltpu.VMEM((3, groups, total * SUB, LANES), jnp.float32),
            pltpu.VMEM((STEPS + 1, groups, (total - 2 * STEPS) * SUB, LANES), jnp.float32),
            pltpu.VMEM((groups, (total - 4 * STEPS) * SUB, LANES), jnp.float32),
            *([plain] * 7),
            pltpu.VMEM(((rows + 1) * SUB, LANES), jnp.float32),
            pltpu.VMEM((rows * SUB, LANES), jnp.float32),
            pltpu.VMEM((7, total, LANES), jnp.float32),
        ],
        60 << 20 if groups > 1 else 32 << 20,
    )(mid_s, mid_a, coef, top, bot)
    outs = [outs[0]] + [swapped(outs[d], d) for d in range(1, count)]
    states, adjoints, gradient = call(
        functools.partial(collect_body, count, wide),
        [(2 * rows, cols), (2 * rows, cols), (rows, cols)],
        [pltpu.VMEM((count, 2 * rows + rows // 2, LANES), jnp.float32)],
    )(*outs)
    return (
        states.reshape(1, 2, rows, cols),
        adjoints.reshape(1, 2, rows, cols),
        gradient,
    )


def solution(mesh):
    placed = (
        P("tm", None, "sx", "sy"),
        P("tm", None, "sx", "sy"),
        P("sx", "sy"),
        P("sx", "sy"),
        P("sx", "sy"),
        P(None, "sx", "sy"),
        P(None, "sx", "sy"),
    )
    return jax.shard_map(
        local,
        mesh=mesh,
        in_specs=placed,
        out_specs=(P("tm", None, "sx", "sy"), P("tm", None, "sx", "sy"), P("sx", "sy")),
        check_vma=False,
    )
```

```python
import functools

import jax
import jax.numpy as jnp
from jax import lax
from jax.experimental import pallas as pl
from jax.experimental.pallas import tpu as pltpu
from jax.sharding import PartitionSpec as P

STEPS = 8
TIME_STEP = 0.1
DIFFUSION = (1.0, 0.4)
DECAY = (1.0, 2.0)

LANES = 128
SUB = 8
PER_GROUP = 4
HALO = 3 * STEPS
HALO_W = 2 * STEPS
SIDE = 32
BLOCK = 8

VMEM_SPEC = pl.BlockSpec(memory_space=pltpu.VMEM)
HBM_SPEC = pl.BlockSpec(memory_space=pltpu.HBM)


def call(body, outs, scratch=(), limit=32 << 20, inputs=None):
    def run(*args):
        return pl.pallas_call(
            body,
            out_shape=[jax.ShapeDtypeStruct(s, jnp.float32) for s in outs],
            in_specs=inputs or [VMEM_SPEC] * len(args),
            out_specs=[VMEM_SPEC] * len(outs),
            scratch_shapes=list(scratch),
            compiler_params=pltpu.CompilerParams(vmem_limit_bytes=limit),
        )(*args)

    return run


def fetch_body(*refs):
    fields, (tile_ref, strip_ref, sems) = refs[:7], refs[7:]
    cols = tile_ref.shape[1]
    copies = []
    at = 0
    for i, ref in enumerate(fields):
        rows = ref.shape[0]
        copies.append(
            pltpu.make_async_copy(ref, tile_ref.at[at : at + rows, :], sems.at[i])
        )
        at += rows
    for copy in copies:
        copy.start()
    for copy in copies:
        copy.wait()
    strip_ref[...] = jnp.where(
        lax.axis_index("sy") == 0, tile_ref[:, cols - LANES :], tile_ref[:, :LANES]
    )


def edges_of(tile_rows):
    return (HALO,) * 5 + (SUB,) * 2


def window_body(count, rows, tile_ref, strip_ref, *refs):
    states, adjoints = refs[:count], refs[count : 2 * count]
    coef_ref, down_ref, up_ref, ext = refs[2 * count :]
    me = lax.axis_index("tm")
    first = lax.axis_index("sy") == 0
    cols = tile_ref.shape[1]
    strip = strip_ref[...]
    zero = jnp.zeros_like(strip)
    ext[:, 0:LANES] = jnp.where(first, zero, strip)
    ext[:, LANES : LANES + cols] = tile_ref[...]
    ext[:, LANES + cols : 2 * LANES + cols] = jnp.where(first, strip, zero)
    wide = cols // count

    def window(lo, hi, t):
        start = LANES - SIDE + wide * t
        base = pl.multiple_of((start // LANES) * LANES, LANES)
        shift = 2 * LANES - start % LANES
        return pltpu.roll(ext[lo:hi, pl.ds(base, 2 * LANES)], shift, 1)[:, :LANES]

    for d in range(count):
        states[d][...] = window(0, 2 * rows, me ^ d)
        adjoints[d][...] = window(2 * rows, 4 * rows, me ^ d)
    coef_ref[...] = window(4 * rows, 11 * rows, me)
    at = 0
    for f, size in enumerate(edges_of(rows)):
        down_ref[at : at + size, :] = coef_ref[(f + 1) * rows - size : (f + 1) * rows, :]
        up_ref[at : at + size, :] = coef_ref[f * rows : f * rows + size, :]
        at += size


def interleave_body(count, halo, *refs):
    cens, (mid, down_ref, up_ref) = refs[:count], refs[count:]
    rows = cens[0].shape[0] // 2
    me = lax.axis_index("tm")
    for d in range(count):
        slab = me ^ d
        g, j = slab // PER_GROUP, slab % PER_GROUP
        for sp in range(2):
            mid[g, pl.ds(sp * PER_GROUP + j, rows, stride=SUB), :] = cens[d][
                sp * rows : (sp + 1) * rows, :
            ]
    size = halo * SUB
    down_ref[...] = mid[:, (rows - halo) * SUB :, :]
    up_ref[...] = mid[:, 0:size, :]


def blocks(lo, hi):
    return [(r, min(r + BLOCK, hi)) for r in range(lo, hi, BLOCK)]


def shift(value, by):
    n = value.shape[0] // SUB
    return pltpu.roll(value.reshape(n, SUB, LANES), by, 1).reshape(n * SUB, LANES)


def at_rows(ref, lo, hi):
    return ref[lo * SUB : hi * SUB, :]


def masked(flag, value):
    return jnp.where(flag, value, jnp.zeros_like(value))


def each_group(groups, fn):
    if groups == 1:
        fn(0)
    else:
        lax.fori_loop(0, groups, lambda g, c: (fn(g), c)[1], 0)


def through_groups(groups, fn, carry):
    if groups == 1:
        fn(0, carry)
    else:
        lax.fori_loop(0, groups, fn, carry)


def slab_of(a, b):
    return lax.broadcasted_iota(jnp.int32, ((b - a) * SUB, LANES), 0) % PER_GROUP


def step(src, dst, lo, hi, off, cv, ce, cd, cx, cq=None):
    for a, b in blocks(lo, hi):
        u = at_rows(src, a - off, b - off)
        e = at_rows(ce, a, b)
        new = (
            at_rows(cd, a, b) * u
            + at_rows(cv, a, b) * at_rows(src, a - off - 1, b - off - 1)
            + at_rows(cv, a + 1, b + 1) * at_rows(src, a - off + 1, b - off + 1)
            + e * pltpu.roll(u, LANES - 1, 1)
            + pltpu.roll(e * u, 1, 1)
            + at_rows(cx, a, b) * shift(u, PER_GROUP)
        )
        if cq is not None:
            new = new + at_rows(cq, a, b)
        dst[(a - off) * SUB : (b - off) * SUB, :] = new


def sweep(groups, work, lo, hi, *coefs):
    def turn(t, carry):
        src = jnp.where(t == 0, 0, 1 + (t + 1) % 2)
        dst = 1 + t % 2
        each_group(groups, lambda g: step(work.at[src, g], work.at[dst, g], lo, hi, 0, *coefs))
        return carry

    lax.fori_loop(0, STEPS, turn, 0)
    return 1 + (STEPS - 1) % 2


def coarse(gd, cx, value, a, b):
    return at_rows(gd, a, b) * value + (STEPS * at_rows(cx, a, b)) * shift(value, PER_GROUP)


def load(groups, work, tile_rows, halo, mid, top_ref, bot_ref):
    s_at = lax.axis_index("sx")
    has_top = s_at > 0
    has_bot = s_at < lax.axis_size("sx") - 1
    end = HALO + tile_rows

    def one(g):
        work[0, g, (HALO - halo) * SUB : HALO * SUB, :] = masked(has_top, top_ref[g])
        work[0, g, HALO * SUB : end * SUB, :] = mid[g]
        work[0, g, end * SUB : (end + halo) * SUB, :] = masked(has_bot, bot_ref[g])

    each_group(groups, one)


def state_body(count, tile_rows, wide, mid, top_ref, bot_ref, coef_ref, ctop_ref, cbot_ref, *rest):
    hist, last_ref, cv, ce, cd, cx, gd, work, cq, tg, flat = rest
    groups = count // PER_GROUP
    total = tile_rows + 2 * HALO
    end = HALO + tile_rows
    me = lax.axis_index("tm")
    s_at = lax.axis_index("sx")
    has_top = s_at > 0
    has_bot = s_at < lax.axis_size("sx") - 1

    at = 0
    fields = []
    for f, size in enumerate(edges_of(tile_rows)):
        flat[f, HALO - size : HALO, :] = masked(has_top, ctop_ref[at : at + size, :])
        flat[f, HALO:end, :] = coef_ref[f * tile_rows : (f + 1) * tile_rows, :]
        flat[f, end : end + size, :] = masked(has_bot, cbot_ref[at : at + size, :])
        fields.append(flat[f])
        at += size
    k, rate, coupling, q0, q1, t0, t1 = fields
    row = lax.broadcasted_iota(jnp.int32, (total, LANES), 0) + (s_at * tile_rows - HALO)
    col = lax.broadcasted_iota(jnp.int32, (total, LANES), 1) + (
        lax.axis_index("sy") * (wide * count) + me * wide - SIDE
    )
    all_rows = tile_rows * lax.axis_size("sx")
    all_cols = wide * count * lax.axis_size("sy")
    half = 0.5 * TIME_STEP
    above = half * (k + pltpu.roll(k, 1, 0))
    below = half * (k + pltpu.roll(k, total - 1, 0))
    east = half * (k + pltpu.roll(k, LANES - 1, 1))
    west = half * (k + pltpu.roll(k, 1, 1))
    faces = above + below + east + west
    above = jnp.where((row >= 1) & (row < all_rows), above, 0.0)
    east = jnp.where((col >= 0) & (col < all_cols - 1), east, 0.0)
    react = TIME_STEP * rate
    cross = react * coupling
    for sp, source in ((0, q0), (1, q1)):
        spread = (
            (cv, DIFFUSION[sp] * above),
            (ce, DIFFUSION[sp] * east),
            (cd, 1.0 - DIFFUSION[sp] * faces - DECAY[sp] * react),
            (cx, cross),
            (cq, TIME_STEP * source),
            (gd, 1.0 - (DECAY[sp] * STEPS) * react),
        )
        for ref, value in spread:
            for j in range(PER_GROUP):
                ref[pl.ds(sp * PER_GROUP + j, total, stride=SUB), :] = value
    tg[pl.ds(PER_GROUP - 1, total, stride=SUB), :] = t0
    tg[pl.ds(SUB - 1, total, stride=SUB), :] = t1

    lo, hi = STEPS, total - STEPS
    load(groups, work, tile_rows, HALO, mid, top_ref, bot_ref)
    last = sweep(groups, work, 1, total - 1, cv, ce, cd, cx, cq)
    for a, b in blocks(lo, hi):
        slab = slab_of(a, b)

        def chain(g, carry, a=a, b=b, slab=slab):
            x = at_rows(work.at[last, g], a, b) - coarse(
                gd, cx, at_rows(work.at[0, g], a, b), a, b
            )
            value = carry
            for _ in range(PER_GROUP - 1):
                value = jnp.where(
                    slab == 0, carry, shift(coarse(gd, cx, value, a, b) + x, 1)
                )
            hist[0, g, (a - lo) * SUB : (b - lo) * SUB, :] = value
            return shift(coarse(gd, cx, value, a, b) + x, SUB - PER_GROUP + 1)

        through_groups(groups, chain, jnp.zeros(((b - a) * SUB, LANES), jnp.float32))

    def forward(t, carry):
        each_group(
            groups,
            lambda g: step(
                hist.at[t, g], hist.at[t + 1, g], lo + 1, hi - 1, lo, cv, ce, cd, cx, cq
            ),
        )
        return carry

    lax.fori_loop(0, STEPS, forward, 0)
    w_lo, w_hi = 2 * STEPS, total - 2 * STEPS
    last_ref[...] = at_rows(hist.at[STEPS, groups - 1], w_lo - lo, w_hi - lo) - at_rows(
        tg, w_lo, w_hi
    )


def adjoint_body(count, tile_rows, mid, top_ref, bot_ref, hist, last_ref, cv, ce, cd, cx, gd, *rest):
    outs = rest[:count]
    work, lag, fv, fh = rest[count:]
    groups = count // PER_GROUP
    total = tile_rows + 2 * HALO
    end = HALO + tile_rows
    lo = STEPS
    me = lax.axis_index("tm")
    load(groups, work, tile_rows, HALO_W, mid, top_ref, bot_ref)
    last = sweep(groups, work, STEPS + 1, total - STEPS - 1, cv, ce, cd, cx)
    w_lo, w_hi = 2 * STEPS, total - 2 * STEPS
    for a, b in blocks(w_lo, w_hi):
        slab = slab_of(a, b)

        def keep(g, a=a, b=b):
            lag[g, (a - w_lo) * SUB : (b - w_lo) * SUB, :] = at_rows(
                work.at[last, g], a, b
            ) - coarse(gd, cx, at_rows(work.at[0, g], a, b), a, b)

        each_group(groups, keep)

        def chain(turn, carry, a=a, b=b, slab=slab):
            g = groups - 1 - turn
            y = lag[g, (a - w_lo) * SUB : (b - w_lo) * SUB, :]
            top = jnp.where(slab == PER_GROUP - 1, carry, 0.0)
            value = top
            for _ in range(PER_GROUP - 1):
                value = jnp.where(
                    slab == PER_GROUP - 1,
                    top,
                    shift(coarse(gd, cx, value, a, b) + y, SUB - 1),
                )
            work[0, g, a * SUB : b * SUB, :] = value
            return shift(coarse(gd, cx, value, a, b) + y, PER_GROUP - 1)

        through_groups(groups, chain, at_rows(last_ref, a - w_lo, b - w_lo))

    lane = lax.broadcasted_iota(jnp.int32, (tile_rows, LANES), 1)
    left = lane < LANES // 2

    def paired(first, second):
        return jnp.where(
            left,
            pltpu.roll(first, LANES - SIDE, 1),
            pltpu.roll(second, LANES // 2 - SIDE, 1),
        )

    for d in range(count):
        slab = me ^ d
        g, j = slab // PER_GROUP, slab % PER_GROUP
        s_rows = [
            hist[0, g, pl.ds((HALO - lo) * SUB + sp * PER_GROUP + j, tile_rows, stride=SUB), :]
            for sp in range(2)
        ]
        w_rows = [
            work[0, g, pl.ds(HALO * SUB + sp * PER_GROUP + j, tile_rows, stride=SUB), :]
            for sp in range(2)
        ]
        outs[d][0:tile_rows, :] = paired(*s_rows)
        outs[d][tile_rows : 2 * tile_rows, :] = paired(*w_rows)

    fv[...] = jnp.zeros_like(fv)
    fh[...] = jnp.zeros_like(fh)

    def products(u, w):
        for a, b in blocks(HALO, end + 1):
            at = slice((a - HALO) * SUB, (b - HALO) * SUB)
            uc, wc = at_rows(u, a - lo, b - lo), at_rows(w, a, b)
            fv[at, :] += (uc - at_rows(u, a - lo - 1, b - lo - 1)) * (
                wc - at_rows(w, a - 1, b - 1)
            )
            if b <= end:
                fh[at, :] += (pltpu.roll(uc, LANES - 1, 1) - uc) * (
                    pltpu.roll(wc, LANES - 1, 1) - wc
                )

    def back(t, carry):
        src = jnp.where(t == 0, 0, 1 + (t + 1) % 2)
        dst = 1 + t % 2

        def one(g):
            products(hist.at[STEPS - 1 - t, g], work.at[src, g])
            step(work.at[src, g], work.at[dst, g], w_lo + 1, w_hi - 1, 0, cv, ce, cd, cx)

        each_group(groups, one)
        return carry

    lax.fori_loop(0, STEPS - 1, back, 0)
    last = 1 + (STEPS - 2) % 2
    each_group(groups, lambda g: products(hist.at[0, g], work.at[last, g]))

    size = tile_rows * SUB
    fh[...] = fv[0:size, :] + fv[SUB : size + SUB, :] + fh[...] + pltpu.roll(fh[...], 1, 1)
    summed = []
    for sp in range(2):
        parts = [
            fh[pl.ds(sp * PER_GROUP + j, tile_rows, stride=SUB), :] for j in range(PER_GROUP)
        ]
        summed.append((parts[0] + parts[1]) + (parts[2] + parts[3]))
    gradient = (-0.5 * TIME_STEP) * (DIFFUSION[0] * summed[0] + DIFFUSION[1] * summed[1])
    middle = tile_rows // 2
    fold = jnp.where(
        left[:middle],
        pltpu.roll(gradient[:middle], LANES - SIDE, 1),
        pltpu.roll(gradient[middle:], LANES // 2 - SIDE, 1),
    )
    for d in range(count):
        outs[d][2 * tile_rows :, :] = fold


def collect_body(count, wide, *refs):
    parts = refs[:count]
    s_ref, w_ref, g_ref, held = refs[count:]
    me = lax.axis_index("tm")
    for d in range(count):
        held[me ^ d] = parts[d][...]
    rows = g_ref.shape[0]
    middle = rows // 2
    per = LANES // wide
    lane = lax.broadcasted_iota(jnp.int32, (rows, LANES), 1)

    def joined(lo, hi, start, v):
        value = None
        for i in range(per):
            t = v * per + i
            piece = held[t, lo:hi, :]
            turn = (i * wide - start) % LANES
            if turn:
                piece = pltpu.roll(piece, turn, 1)
            value = piece if i == 0 else jnp.where(lane[: hi - lo] >= i * wide, piece, value)
        return value

    for v in range(count // per):
        at = slice(v * LANES, (v + 1) * LANES)
        for sp in range(2):
            start = sp * (LANES // 2)
            s_ref[sp * rows : (sp + 1) * rows, at] = joined(0, rows, start, v)
            w_ref[sp * rows : (sp + 1) * rows, at] = joined(rows, 2 * rows, start, v)
            g_ref[sp * middle : (sp + 1) * middle, at] = joined(
                2 * rows, 2 * rows + middle, start, v
            )


def local(state_guess, adjoint_guess, diffusivity, decay_rate, coupling, control, target):
    rows, cols = diffusivity.shape
    count = lax.axis_size("tm")
    groups = count // PER_GROUP
    wide = cols // count
    total = rows + 2 * HALO
    fields = (
        state_guess.reshape(2 * rows, cols),
        adjoint_guess.reshape(2 * rows, cols),
        diffusivity,
        decay_rate,
        coupling,
        control.reshape(2 * rows, cols),
        target.reshape(2 * rows, cols),
    )

    def exchanged(parts):
        return [parts[0]] + [
            lax.ppermute(parts[d], "tm", [(i, i ^ d) for i in range(count)])
            for d in range(1, count)
        ]

    def turned(down, up):
        n = lax.axis_size("sx")
        return (
            lax.ppermute(down, "sx", [(i, (i + 1) % n) for i in range(n)]),
            lax.ppermute(up, "sx", [((i + 1) % n, i) for i in range(n)]),
        )

    tile, strip = call(
        fetch_body,
        [(11 * rows, cols), (11 * rows, LANES)],
        [pltpu.SemaphoreType.DMA((7,))],
        inputs=[HBM_SPEC] * 7,
    )(*[pltpu.with_memory_space_constraint(f, pltpu.HBM) for f in fields])
    strip = lax.ppermute(strip, "sy", [(0, 1), (1, 0)])
    edge = (sum(edges_of(rows)), LANES)
    windows = call(
        functools.partial(window_body, count, rows),
        [(2 * rows, LANES)] * (2 * count) + [(7 * rows, LANES), edge, edge],
        [pltpu.VMEM((11 * rows, cols + 2 * LANES), jnp.float32)],
    )(tile, strip)
    coef, down, up = windows[2 * count :]
    states = exchanged(windows[:count])
    adjoints = exchanged(windows[count : 2 * count])
    coef_halo = turned(down, up)

    def interleaved(parts, halo):
        mid, down, up = call(
            functools.partial(interleave_body, count, halo),
            [(groups, rows * SUB, LANES)] + [(groups, halo * SUB, LANES)] * 2,
        )(*parts)
        return (mid, *turned(down, up))

    plain = (total * SUB, LANES)
    work = pltpu.VMEM((3, groups, total * SUB, LANES), jnp.float32)
    limit = 60 << 20 if groups > 1 else 32 << 20
    kept = call(
        functools.partial(state_body, count, rows, wide),
        [
            (STEPS + 1, groups, (total - 2 * STEPS) * SUB, LANES),
            ((total - 4 * STEPS) * SUB, LANES),
            *([plain] * 5),
        ],
        [
            work,
            pltpu.VMEM(plain, jnp.float32),
            pltpu.VMEM(plain, jnp.float32),
            pltpu.VMEM((7, total, LANES), jnp.float32),
        ],
        limit,
    )(*interleaved(states, HALO), coef, *coef_halo)
    outs = call(
        functools.partial(adjoint_body, count, rows),
        [(2 * rows + rows // 2, LANES)] * count,
        [
            work,
            pltpu.VMEM((groups, (total - 4 * STEPS) * SUB, LANES), jnp.float32),
            pltpu.VMEM(((rows + 1) * SUB, LANES), jnp.float32),
            pltpu.VMEM((rows * SUB, LANES), jnp.float32),
        ],
        limit,
    )(*interleaved(adjoints, HALO_W), *kept)
    outs = exchanged(outs)
    states, adjoints, gradient = call(
        functools.partial(collect_body, count, wide),
        [(2 * rows, cols), (2 * rows, cols), (rows, cols)],
        [pltpu.VMEM((count, 2 * rows + rows // 2, LANES), jnp.float32)],
    )(*outs)
    return (
        states.reshape(1, 2, rows, cols),
        adjoints.reshape(1, 2, rows, cols),
        gradient,
    )


def solution(mesh):
    placed = (
        P("tm", None, "sx", "sy"),
        P("tm", None, "sx", "sy"),
        P("sx", "sy"),
        P("sx", "sy"),
        P("sx", "sy"),
        P(None, "sx", "sy"),
        P(None, "sx", "sy"),
    )
    return jax.shard_map(
        local,
        mesh=mesh,
        in_specs=placed,
        out_specs=(P("tm", None, "sx", "sy"), P("tm", None, "sx", "sy"), P("sx", "sy")),
        check_vma=False,
    )
```

```python
import functools

import jax
import jax.numpy as jnp
from jax import lax
from jax.experimental import pallas as pl
from jax.experimental.pallas import tpu as pltpu
from jax.sharding import PartitionSpec as P

STEPS = 8
TIME_STEP = 0.1
DIFFUSION = (1.0, 0.4)
DECAY = (1.0, 2.0)

LANES = 128
SUB = 8
PER_GROUP = 4
HALO = 3 * STEPS
HALO_W = 2 * STEPS
SIDE = 32
BLOCK = 8

VMEM_SPEC = pl.BlockSpec(memory_space=pltpu.VMEM)
HBM_SPEC = pl.BlockSpec(memory_space=pltpu.HBM)


def call(body, outs, scratch=(), limit=32 << 20, inputs=None):
    def run(*args):
        return pl.pallas_call(
            body,
            out_shape=[jax.ShapeDtypeStruct(s, jnp.float32) for s in outs],
            in_specs=inputs or [VMEM_SPEC] * len(args),
            out_specs=[VMEM_SPEC] * len(outs),
            scratch_shapes=list(scratch),
            compiler_params=pltpu.CompilerParams(vmem_limit_bytes=limit),
        )(*args)

    return run


def fetch_body(*refs):
    fields, (tile_ref, strip_ref, sems) = refs[:7], refs[7:]
    cols = tile_ref.shape[1]
    copies = []
    at = 0
    for i, ref in enumerate(fields):
        rows = ref.shape[0]
        copies.append(
            pltpu.make_async_copy(ref, tile_ref.at[at : at + rows, :], sems.at[i])
        )
        at += rows
    for copy in copies:
        copy.start()
    for copy in copies:
        copy.wait()
    strip_ref[...] = jnp.where(
        lax.axis_index("sy") == 0, tile_ref[:, cols - LANES :], tile_ref[:, :LANES]
    )


def edges_of(tile_rows):
    return (HALO,) * 5 + (SUB,) * 2


def extend(ext, lo, hi, tile, strip):
    first = lax.axis_index("sy") == 0
    cols = tile.shape[1]
    zero = jnp.zeros_like(strip)
    ext[lo:hi, 0:LANES] = jnp.where(first, zero, strip)
    ext[lo:hi, LANES : LANES + cols] = tile
    ext[lo:hi, LANES + cols : 2 * LANES + cols] = jnp.where(first, strip, zero)


def window(ext, lo, hi, start):
    start = start + LANES - SIDE
    base = pl.multiple_of((start // LANES) * LANES, LANES)
    turn = 2 * LANES - start % LANES
    return pltpu.roll(ext[lo:hi, pl.ds(base, 2 * LANES)], turn, 1)[:, :LANES]


def window_body(count, rows, tile_ref, strip_ref, *refs):
    states, (coef_ref, down_ref, up_ref, ext) = refs[:count], refs[count:]
    me = lax.axis_index("tm")
    cols = tile_ref.shape[1]
    wide = cols // count
    extend(ext, 0, 11 * rows, tile_ref[...], strip_ref[...])
    for d in range(count):
        states[d][...] = window(ext, 0, 2 * rows, wide * (me ^ d))
    coef_ref[...] = window(ext, 4 * rows, 11 * rows, wide * me)
    at = 0
    for f, size in enumerate(edges_of(rows)):
        down_ref[at : at + size, :] = coef_ref[(f + 1) * rows - size : (f + 1) * rows, :]
        up_ref[at : at + size, :] = coef_ref[f * rows : f * rows + size, :]
        at += size
    for sp in range(2):
        lo = (2 + sp) * rows
        for ref, low in ((down_ref, lo + rows - HALO_W), (up_ref, lo)):
            here = slice(low, low + HALO_W)
            for i in range(cols // LANES):
                ref[at + i * HALO_W : at + (i + 1) * HALO_W, :] = tile_ref[
                    here, i * LANES : (i + 1) * LANES
                ]
            i = cols // LANES
            ref[at + i * HALO_W : at + (i + 1) * HALO_W, :] = strip_ref[here, :]
        at += (cols // LANES + 1) * HALO_W


def adjoint_window_body(count, rows, tile_ref, strip_ref, top_ref, bot_ref, after, *refs):
    del after
    outs, ext = refs[:count], refs[count]
    me = lax.axis_index("tm")
    s_at = lax.axis_index("sx")
    cols = tile_ref.shape[1]
    wide = cols // count
    tall = rows + 2 * HALO_W
    for sp in range(2):
        lo = (2 + sp) * rows
        base = sp * tall
        at = sum(edges_of(rows)) + sp * (cols // LANES + 1) * HALO_W
        extend(
            ext,
            base + HALO_W,
            base + HALO_W + rows,
            tile_ref[lo : lo + rows, :],
            strip_ref[lo : lo + rows, :],
        )
        for ref, start, flag in (
            (top_ref, base, s_at > 0),
            (bot_ref, base + HALO_W + rows, s_at < lax.axis_size("sx") - 1),
        ):
            parts = [
                masked(flag, ref[at + i * HALO_W : at + (i + 1) * HALO_W, :])
                for i in range(cols // LANES + 1)
            ]
            extend(
                ext, start, start + HALO_W, jnp.concatenate(parts[:-1], axis=1), parts[-1]
            )
    for d in range(count):
        outs[d][...] = window(ext, 0, 2 * tall, wide * (me ^ d))


def interleave_body(count, halo, *refs):
    cens, (mid, down_ref, up_ref) = refs[:count], refs[count:]
    rows = cens[0].shape[0] // 2
    me = lax.axis_index("tm")
    for d in range(count):
        slab = me ^ d
        g, j = slab // PER_GROUP, slab % PER_GROUP
        for sp in range(2):
            mid[g, pl.ds(sp * PER_GROUP + j, rows, stride=SUB), :] = cens[d][
                sp * rows : (sp + 1) * rows, :
            ]
    size = halo * SUB
    down_ref[...] = mid[:, (rows - halo) * SUB :, :]
    up_ref[...] = mid[:, 0:size, :]


def blocks(lo, hi):
    return [(r, min(r + BLOCK, hi)) for r in range(lo, hi, BLOCK)]


def shift(value, by):
    n = value.shape[0] // SUB
    return pltpu.roll(value.reshape(n, SUB, LANES), by, 1).reshape(n * SUB, LANES)


def at_rows(ref, lo, hi):
    return ref[lo * SUB : hi * SUB, :]


def masked(flag, value):
    return jnp.where(flag, value, jnp.zeros_like(value))


def each_group(groups, fn):
    if groups == 1:
        fn(0)
    else:
        lax.fori_loop(0, groups, lambda g, c: (fn(g), c)[1], 0)


def through_groups(groups, fn, carry):
    if groups == 1:
        fn(0, carry)
    else:
        lax.fori_loop(0, groups, fn, carry)


def slab_of(a, b):
    return lax.broadcasted_iota(jnp.int32, ((b - a) * SUB, LANES), 0) % PER_GROUP


def step(src, dst, lo, hi, coefs, seen=None):
    cv, ce, cd, cx = coefs[:4]
    for a, b in blocks(lo, hi):
        n = (b - a) * SUB
        rows = at_rows(src, a - 1, b + 1)
        face = at_rows(cv, a, b + 1)
        u = rows[SUB : SUB + n]
        e = at_rows(ce, a, b)
        east = pltpu.roll(u, LANES - 1, 1)
        new = at_rows(cd, a, b) * u + face[:n] * rows[:n] + face[SUB:] * rows[2 * SUB :]
        if len(coefs) > 4:
            new = new + at_rows(coefs[4], a, b)
        new = new + (e * east + pltpu.roll(e * u, 1, 1))
        new = new + at_rows(cx, a, b) * shift(u, PER_GROUP)
        dst[a * SUB : b * SUB, :] = new
        if seen is not None:
            seen(a, b, rows[:n], u, east, new)


def sweep(groups, one, two, lo, hi, coefs):
    def turn(t, carry):
        def run(g):
            step(one.at[g], two.at[g], lo, hi, coefs)
            step(two.at[g], one.at[g], lo, hi, coefs)

        each_group(groups, run)
        return carry

    lax.fori_loop(0, STEPS // 2, turn, 0)


def coarse(gd, cx, value, a, b):
    return at_rows(gd, a, b) * value + (STEPS * at_rows(cx, a, b)) * shift(value, PER_GROUP)


def load(groups, refs, tile_rows, halo, mid, top_ref, bot_ref):
    s_at = lax.axis_index("sx")
    has_top = s_at > 0
    has_bot = s_at < lax.axis_size("sx") - 1
    end = HALO + tile_rows

    def one(g):
        for ref in refs:
            ref[g, (HALO - halo) * SUB : HALO * SUB, :] = masked(has_top, top_ref[g])
            ref[g, HALO * SUB : end * SUB, :] = mid[g]
            ref[g, end * SUB : (end + halo) * SUB, :] = masked(has_bot, bot_ref[g])

    each_group(groups, one)


def coef_body(count, tile_rows, wide, coef_ref, ctop_ref, cbot_ref, *rest):
    cv, ce, cd, cx, cq, gd, tg, flat = rest
    total = tile_rows + 2 * HALO
    end = HALO + tile_rows
    me = lax.axis_index("tm")
    s_at = lax.axis_index("sx")
    has_top = s_at > 0
    has_bot = s_at < lax.axis_size("sx") - 1
    at = 0
    fields = []
    for f, size in enumerate(edges_of(tile_rows)):
        flat[f, HALO - size : HALO, :] = masked(has_top, ctop_ref[at : at + size, :])
        flat[f, HALO:end, :] = coef_ref[f * tile_rows : (f + 1) * tile_rows, :]
        flat[f, end : end + size, :] = masked(has_bot, cbot_ref[at : at + size, :])
        fields.append(flat[f])
        at += size
    k, rate, coupling, q0, q1, t0, t1 = fields
    row = lax.broadcasted_iota(jnp.int32, (total, LANES), 0) + (s_at * tile_rows - HALO)
    col = lax.broadcasted_iota(jnp.int32, (total, LANES), 1) + (
        lax.axis_index("sy") * (wide * count) + me * wide - SIDE
    )
    all_rows = tile_rows * lax.axis_size("sx")
    all_cols = wide * count * lax.axis_size("sy")
    half = 0.5 * TIME_STEP
    above = half * (k + pltpu.roll(k, 1, 0))
    below = half * (k + pltpu.roll(k, total - 1, 0))
    east = half * (k + pltpu.roll(k, LANES - 1, 1))
    west = half * (k + pltpu.roll(k, 1, 1))
    faces = above + below + east + west
    above = jnp.where((row >= 1) & (row < all_rows), above, 0.0)
    east = jnp.where((col >= 0) & (col < all_cols - 1), east, 0.0)
    react = TIME_STEP * rate
    cross = react * coupling
    for sp, source in ((0, q0), (1, q1)):
        spread = (
            (cv, DIFFUSION[sp] * above),
            (ce, DIFFUSION[sp] * east),
            (cd, 1.0 - DIFFUSION[sp] * faces - DECAY[sp] * react),
            (cx, cross),
            (cq, TIME_STEP * source),
            (gd, 1.0 - (DECAY[sp] * STEPS) * react),
            (tg, (t0, t1)[sp]),
        )
        for ref, value in spread:
            for j in range(PER_GROUP):
                ref[pl.ds(sp * PER_GROUP + j, total, stride=SUB), :] = value


def state_body(
    count, tile_rows, mid, top_ref, bot_ref, cv, ce, cd, cx, cq, gd, tg, hist, slope, last_ref, *rest
):
    guess, one, two = rest
    groups = count // PER_GROUP
    total = tile_rows + 2 * HALO
    coefs = (cv, ce, cd, cx, cq)
    lo, hi = STEPS, total - STEPS
    load(groups, (guess, one), tile_rows, HALO, mid, top_ref, bot_ref)
    sweep(groups, one, two, 1, total - 1, coefs)
    for a, b in blocks(lo, hi):
        slab = slab_of(a, b)

        def chain(g, carry, a=a, b=b, slab=slab):
            x = at_rows(one.at[g], a, b) - coarse(gd, cx, at_rows(guess.at[g], a, b), a, b)
            value = carry
            for _ in range(PER_GROUP - 1):
                value = jnp.where(
                    slab == 0, carry, shift(coarse(gd, cx, value, a, b) + x, 1)
                )
            two[g, a * SUB : b * SUB, :] = value
            return shift(coarse(gd, cx, value, a, b) + x, SUB - PER_GROUP + 1)

        through_groups(groups, chain, jnp.zeros(((b - a) * SUB, LANES), jnp.float32))

    def forward(turn, carry):
        def run(g):
            for k, (src, dst) in enumerate(((two, one), (one, two))):
                t = 2 * turn + k

                def seen(a, b, before, here, east, new, t=t):
                    hist[t, g, (a - lo) * SUB : (b - lo) * SUB, :] = here
                    if HALO <= a < HALO + tile_rows:
                        at = slice((a - HALO) * SUB, (b - HALO) * SUB)
                        slope[t, g, at, :] = east - here

                step(src.at[g], dst.at[g], lo, hi, coefs, seen)

        each_group(groups, run)
        return carry

    lax.fori_loop(0, STEPS // 2, forward, 0)
    w_lo, w_hi = 2 * STEPS, total - 2 * STEPS
    last_ref[...] = at_rows(two.at[groups - 1], w_lo, w_hi) - at_rows(tg, w_lo, w_hi)


def lag_body(count, tile_rows, *refs):
    cens, (cv, ce, cd, cx, gd, lag, guess, one, two) = refs[:count], refs[count:]
    groups = count // PER_GROUP
    total = tile_rows + 2 * HALO
    tall = tile_rows + 2 * HALO_W
    me = lax.axis_index("tm")
    for d in range(count):
        slab = me ^ d
        g, j = slab // PER_GROUP, slab % PER_GROUP
        for sp in range(2):
            start = (HALO - HALO_W) * SUB + sp * PER_GROUP + j
            value = cens[d][sp * tall : (sp + 1) * tall, :]
            guess[g, pl.ds(start, tall, stride=SUB), :] = value
            one[g, pl.ds(start, tall, stride=SUB), :] = value
    sweep(groups, one, two, STEPS + 1, total - STEPS - 1, (cv, ce, cd, cx))
    w_lo, w_hi = 2 * STEPS, total - 2 * STEPS

    def run(g):
        for a, b in blocks(w_lo, w_hi):
            lag[g, (a - w_lo) * SUB : (b - w_lo) * SUB, :] = at_rows(
                one.at[g], a, b
            ) - coarse(gd, cx, at_rows(guess.at[g], a, b), a, b)

    each_group(groups, run)


def adjoint_body(count, tile_rows, lag, hist, slope, last_ref, cv, ce, cd, cx, gd, *rest):
    outs = rest[:count]
    one, two, fv, fh = rest[count:]
    groups = count // PER_GROUP
    total = tile_rows + 2 * HALO
    end = HALO + tile_rows
    coefs = (cv, ce, cd, cx)
    lo = STEPS
    me = lax.axis_index("tm")
    w_lo, w_hi = 2 * STEPS, total - 2 * STEPS
    for a, b in blocks(w_lo, w_hi):
        slab = slab_of(a, b)

        def chain(turn, carry, a=a, b=b, slab=slab):
            g = groups - 1 - turn
            y = lag[g, (a - w_lo) * SUB : (b - w_lo) * SUB, :]
            top = jnp.where(slab == PER_GROUP - 1, carry, 0.0)
            value = top
            for _ in range(PER_GROUP - 1):
                value = jnp.where(
                    slab == PER_GROUP - 1,
                    top,
                    shift(coarse(gd, cx, value, a, b) + y, SUB - 1),
                )
            two[g, a * SUB : b * SUB, :] = value
            return shift(coarse(gd, cx, value, a, b) + y, PER_GROUP - 1)

        through_groups(groups, chain, at_rows(last_ref, a - w_lo, b - w_lo))

    def clear(g):
        for r in (w_lo - 1, w_hi):
            for ref in (one, two):
                ref[g, r * SUB : (r + 1) * SUB, :] = jnp.zeros((SUB, LANES), jnp.float32)

    each_group(groups, clear)

    lane = lax.broadcasted_iota(jnp.int32, (tile_rows, LANES), 1)
    left = lane < LANES // 2

    def paired(first, second):
        return jnp.where(
            left,
            pltpu.roll(first, LANES - SIDE, 1),
            pltpu.roll(second, LANES // 2 - SIDE, 1),
        )

    for d in range(count):
        slab = me ^ d
        g, j = slab // PER_GROUP, slab % PER_GROUP
        s_rows = [
            hist[0, g, pl.ds((HALO - lo) * SUB + sp * PER_GROUP + j, tile_rows, stride=SUB), :]
            for sp in range(2)
        ]
        w_rows = [
            two[g, pl.ds(HALO * SUB + sp * PER_GROUP + j, tile_rows, stride=SUB), :]
            for sp in range(2)
        ]
        outs[d][0:tile_rows, :] = paired(*s_rows)
        outs[d][tile_rows : 2 * tile_rows, :] = paired(*w_rows)

    fv[...] = jnp.zeros_like(fv)
    fh[...] = jnp.zeros_like(fh)

    def back(turn, carry):
        def run(g):
            for k, (src, dst) in enumerate(((two, one), (one, two))):
                t = STEPS - 1 - 2 * turn - k

                def seen(a, b, before, here, east, new, t=t):
                    if a < HALO or a > end:
                        return
                    at = slice((a - HALO) * SUB, (b - HALO) * SUB)
                    u = hist[t, g, (a - lo - 1) * SUB : (b - lo) * SUB, :]
                    fv[at, :] += (u[SUB:] - u[:-SUB]) * (here - before)
                    if b <= end:
                        fh[at, :] += slope[t, g, at, :] * (
                            east - here
                        )

                step(src.at[g], dst.at[g], w_lo, w_hi, coefs, seen)

        each_group(groups, run)
        return carry

    lax.fori_loop(0, STEPS // 2, back, 0)

    size = tile_rows * SUB
    fh[...] = fv[0:size, :] + fv[SUB : size + SUB, :] + fh[...] + pltpu.roll(fh[...], 1, 1)
    summed = []
    for sp in range(2):
        parts = [
            fh[pl.ds(sp * PER_GROUP + j, tile_rows, stride=SUB), :] for j in range(PER_GROUP)
        ]
        summed.append((parts[0] + parts[1]) + (parts[2] + parts[3]))
    gradient = (-0.5 * TIME_STEP) * (DIFFUSION[0] * summed[0] + DIFFUSION[1] * summed[1])
    middle = tile_rows // 2
    fold = jnp.where(
        left[:middle],
        pltpu.roll(gradient[:middle], LANES - SIDE, 1),
        pltpu.roll(gradient[middle:], LANES // 2 - SIDE, 1),
    )
    for d in range(count):
        outs[d][2 * tile_rows :, :] = fold


def collect_body(count, wide, *refs):
    parts = refs[:count]
    s_ref, w_ref, g_ref, held = refs[count:]
    me = lax.axis_index("tm")
    for d in range(count):
        held[me ^ d] = parts[d][...]
    rows = g_ref.shape[0]
    middle = rows // 2
    per = LANES // wide
    lane = lax.broadcasted_iota(jnp.int32, (rows, LANES), 1)

    def joined(lo, hi, start, v):
        value = None
        for i in range(per):
            t = v * per + i
            piece = held[t, lo:hi, :]
            turn = (i * wide - start) % LANES
            if turn:
                piece = pltpu.roll(piece, turn, 1)
            value = piece if i == 0 else jnp.where(lane[: hi - lo] >= i * wide, piece, value)
        return value

    for v in range(count // per):
        at = slice(v * LANES, (v + 1) * LANES)
        for sp in range(2):
            start = sp * (LANES // 2)
            s_ref[sp * rows : (sp + 1) * rows, at] = joined(0, rows, start, v)
            w_ref[sp * rows : (sp + 1) * rows, at] = joined(rows, 2 * rows, start, v)
            g_ref[sp * middle : (sp + 1) * middle, at] = joined(
                2 * rows, 2 * rows + middle, start, v
            )


def local(state_guess, adjoint_guess, diffusivity, decay_rate, coupling, control, target):
    rows, cols = diffusivity.shape
    count = lax.axis_size("tm")
    groups = count // PER_GROUP
    wide = cols // count
    total = rows + 2 * HALO
    fields = (
        state_guess.reshape(2 * rows, cols),
        adjoint_guess.reshape(2 * rows, cols),
        diffusivity,
        decay_rate,
        coupling,
        control.reshape(2 * rows, cols),
        target.reshape(2 * rows, cols),
    )

    def exchanged(parts):
        return [parts[0]] + [
            lax.ppermute(parts[d], "tm", [(i, i ^ d) for i in range(count)])
            for d in range(1, count)
        ]

    def turned(down, up):
        n = lax.axis_size("sx")
        return (
            lax.ppermute(down, "sx", [(i, (i + 1) % n) for i in range(n)]),
            lax.ppermute(up, "sx", [((i + 1) % n, i) for i in range(n)]),
        )

    tile, strip = call(
        fetch_body,
        [(11 * rows, cols), (11 * rows, LANES)],
        [pltpu.SemaphoreType.DMA((7,))],
        inputs=[HBM_SPEC] * 7,
    )(*[pltpu.with_memory_space_constraint(f, pltpu.HBM) for f in fields])
    strip = lax.ppermute(strip, "sy", [(0, 1), (1, 0)])
    pieces = cols // LANES + 1
    edge = (sum(edges_of(rows)) + 2 * pieces * HALO_W, LANES)
    *windows, coef, down, up = call(
        functools.partial(window_body, count, rows),
        [(2 * rows, LANES)] * count + [(7 * rows, LANES), edge, edge],
        [pltpu.VMEM((11 * rows, cols + 2 * LANES), jnp.float32)],
    )(tile, strip)
    states = exchanged(windows)
    edges = turned(down, up)
    mid, down, up = call(
        functools.partial(interleave_body, count, HALO),
        [(groups, rows * SUB, LANES)] + [(groups, HALO * SUB, LANES)] * 2,
    )(*states)
    state_edges = turned(down, up)
    tall = rows + 2 * HALO_W
    windows = call(
        functools.partial(adjoint_window_body, count, rows),
        [(2 * tall, LANES)] * count,
        [pltpu.VMEM((2 * tall, cols + 2 * LANES), jnp.float32)],
    )(tile, strip, *edges, mid)
    adjoints = exchanged(windows)
    plain = (total * SUB, LANES)
    work = pltpu.VMEM((groups, total * SUB, LANES), jnp.float32)
    limit = 60 << 20 if groups > 1 else 32 << 20
    *coefs, gd, tg = call(
        functools.partial(coef_body, count, rows, wide),
        [plain] * 7,
        [pltpu.VMEM((7, total, LANES), jnp.float32)],
    )(coef, *edges)
    (lag,) = call(
        functools.partial(lag_body, count, rows),
        [(groups, (total - 4 * STEPS) * SUB, LANES)],
        [work] * 3,
        limit,
    )(*adjoints, *coefs[:4], gd)
    hist, slope, last = call(
        functools.partial(state_body, count, rows),
        [
            (STEPS, groups, (total - 2 * STEPS) * SUB, LANES),
            (STEPS, groups, rows * SUB, LANES),
            ((total - 4 * STEPS) * SUB, LANES),
        ],
        [work] * 3,
        limit,
    )(mid, *state_edges, *coefs, gd, tg)
    outs = call(
        functools.partial(adjoint_body, count, rows),
        [(2 * rows + rows // 2, LANES)] * count,
        [
            *([work] * 2),
            pltpu.VMEM(((rows + BLOCK) * SUB, LANES), jnp.float32),
            pltpu.VMEM((rows * SUB, LANES), jnp.float32),
        ],
        limit,
    )(lag, hist, slope, last, *coefs[:4], gd)
    outs = exchanged(outs)
    states, adjoints, gradient = call(
        functools.partial(collect_body, count, wide),
        [(2 * rows, cols), (2 * rows, cols), (rows, cols)],
        [pltpu.VMEM((count, 2 * rows + rows // 2, LANES), jnp.float32)],
    )(*outs)
    return (
        states.reshape(1, 2, rows, cols),
        adjoints.reshape(1, 2, rows, cols),
        gradient,
    )


def solution(mesh):
    placed = (
        P("tm", None, "sx", "sy"),
        P("tm", None, "sx", "sy"),
        P("sx", "sy"),
        P("sx", "sy"),
        P("sx", "sy"),
        P(None, "sx", "sy"),
        P(None, "sx", "sy"),
    )
    return jax.shard_map(
        local,
        mesh=mesh,
        in_specs=placed,
        out_specs=(P("tm", None, "sx", "sy"), P("tm", None, "sx", "sy"), P("sx", "sy")),
        check_vma=False,
    )
```

```python
import functools

import jax
import jax.numpy as jnp
from jax import lax
from jax.experimental import pallas as pl
from jax.experimental.pallas import tpu as pltpu
from jax.sharding import PartitionSpec as P

STEPS = 8
TIME_STEP = 0.1
DIFFUSION = (1.0, 0.4)
DECAY = (1.0, 2.0)

LANES = 128
SUB = 8
PER_GROUP = 4
HALO = 3 * STEPS
HALO_W = 2 * STEPS
SIDE = 32
BLOCK = 8

VMEM_SPEC = pl.BlockSpec(memory_space=pltpu.VMEM)
HBM_SPEC = pl.BlockSpec(memory_space=pltpu.HBM)


def call(body, outs, scratch=(), limit=32 << 20, inputs=None):
    def run(*args):
        return pl.pallas_call(
            body,
            out_shape=[jax.ShapeDtypeStruct(s, jnp.float32) for s in outs],
            in_specs=inputs or [VMEM_SPEC] * len(args),
            out_specs=[VMEM_SPEC] * len(outs),
            scratch_shapes=list(scratch),
            compiler_params=pltpu.CompilerParams(vmem_limit_bytes=limit),
        )(*args)

    return run


def fetch_body(*refs):
    fields, (tile_ref, strip_ref, sems) = refs[:7], refs[7:]
    cols = tile_ref.shape[1]
    copies = []
    at = 0
    for i, ref in enumerate(fields):
        rows = ref.shape[0]
        copies.append(
            pltpu.make_async_copy(ref, tile_ref.at[at : at + rows, :], sems.at[i])
        )
        at += rows
    for copy in copies:
        copy.start()
    for copy in copies:
        copy.wait()
    strip_ref[...] = jnp.where(
        lax.axis_index("sy") == 0, tile_ref[:, cols - LANES :], tile_ref[:, :LANES]
    )


EARLY = (HALO,) * 2
LATE = (HALO,) * 3 + (SUB,) * 2


def edge_rows(refs, coef_ref, first, sizes, at):
    down_ref, up_ref = refs
    rows = coef_ref.shape[0] // 7
    for f, size in enumerate(sizes, first):
        down_ref[at : at + size, :] = coef_ref[(f + 1) * rows - size : (f + 1) * rows, :]
        up_ref[at : at + size, :] = coef_ref[f * rows : f * rows + size, :]
        at += size
    return at


def joined_rows(flat, coef_ref, refs, first, sizes, at):
    s_at = lax.axis_index("sx")
    has_top = s_at > 0
    has_bot = s_at < lax.axis_size("sx") - 1
    top_ref, bot_ref = refs
    rows = coef_ref.shape[0] // 7
    end = HALO + rows
    fields = []
    for i, size in enumerate(sizes):
        f = first + i
        flat[i, HALO - size : HALO, :] = masked(has_top, top_ref[at : at + size, :])
        flat[i, HALO:end, :] = coef_ref[f * rows : (f + 1) * rows, :]
        flat[i, end : end + size, :] = masked(has_bot, bot_ref[at : at + size, :])
        fields.append(flat[i])
        at += size
    return fields


def extend(ext, lo, hi, tile, strip):
    first = lax.axis_index("sy") == 0
    cols = tile.shape[1]
    zero = jnp.zeros_like(strip)
    ext[lo:hi, 0:LANES] = jnp.where(first, zero, strip)
    ext[lo:hi, LANES : LANES + cols] = tile
    ext[lo:hi, LANES + cols : 2 * LANES + cols] = jnp.where(first, strip, zero)


def window(ext, lo, hi, start):
    start = start + LANES - SIDE
    base = pl.multiple_of((start // LANES) * LANES, LANES)
    turn = 2 * LANES - start % LANES
    return pltpu.roll(ext[lo:hi, pl.ds(base, 2 * LANES)], turn, 1)[:, :LANES]


def window_body(count, rows, tile_ref, strip_ref, *refs):
    outs, ext = refs[:count], refs[count]
    me = lax.axis_index("tm")
    wide = tile_ref.shape[1] // count
    extend(ext, 0, 2 * rows, tile_ref[: 2 * rows, :], strip_ref[: 2 * rows, :])
    for d in range(count):
        outs[d][...] = window(ext, 0, 2 * rows, wide * (me ^ d))


def edge_body(count, rows, tile_ref, strip_ref, after, coef_ref, down_ref, up_ref, ext):
    del after
    me = lax.axis_index("tm")
    cols = tile_ref.shape[1]
    extend(ext, 0, 7 * rows, tile_ref[4 * rows :, :], strip_ref[4 * rows :, :])
    coef_ref[...] = window(ext, 0, 7 * rows, cols // count * me)
    at = edge_rows((down_ref, up_ref), coef_ref, 0, EARLY, 0)
    lane = lax.broadcasted_iota(jnp.int32, (SUB, LANES), 1)
    for ref, low in ((down_ref, rows - HALO_W), (up_ref, 0)):
        put, sides = at, None
        for sp in range(2):
            here = (2 + sp) * rows + low
            for i in range(cols // LANES):
                ref[put : put + HALO_W, :] = tile_ref[
                    here : here + HALO_W, i * LANES : (i + 1) * LANES
                ]
                put += HALO_W
            for i in range(HALO_W // SUB):
                strip = strip_ref[here + i * SUB : here + (i + 1) * SUB, :]
                n = sp * (HALO_W // SUB) + i
                strip = jnp.where(
                    lax.axis_index("sy") == 0,
                    pltpu.roll(strip, n * SIDE, 1),
                    pltpu.roll(strip, (n + 1) * SIDE % LANES, 1),
                )
                sides = strip if n == 0 else jnp.where(lane >= n * SIDE, strip, sides)
        ref[put : put + SUB, :] = sides


PACKED = 3 * LANES // 4


def packed(value):
    n = value.shape[0] // 4
    cut = (LANES - PACKED) // 2
    lane = lax.broadcasted_iota(jnp.int32, (n, LANES), 1)
    last = value[3 * n :]
    parts = []
    for i in range(3):
        main = pltpu.roll(value[i * n : (i + 1) * n], LANES - cut, 1)
        rest = pltpu.roll(last, (PACKED - cut - i * (LANES - PACKED)) % LANES, 1)
        parts.append(jnp.where(lane < PACKED, main, rest))
    return jnp.concatenate(parts, axis=0)


def unpacked(value):
    n = value.shape[0] // 3
    cut = (LANES - PACKED) // 2
    side = LANES - PACKED
    lane = lax.broadcasted_iota(jnp.int32, (n, LANES), 1)
    parts, last = [], None
    for i in range(3):
        part = value[i * n : (i + 1) * n]
        parts.append(pltpu.roll(part, cut, 1))
        rest = pltpu.roll(part, (cut + i * side - PACKED) % LANES, 1)
        last = rest if i == 0 else jnp.where(lane >= cut + i * side, rest, last)
    return jnp.concatenate([*parts, last], axis=0)


def adjoint_window_body(count, rows, tile_ref, strip_ref, top_ref, bot_ref, after, *refs):
    del after
    outs, ext = refs[:count], refs[count]
    me = lax.axis_index("tm")
    s_at = lax.axis_index("sx")
    cols = tile_ref.shape[1]
    wide = cols // count
    tall = rows + 2 * HALO_W
    for sp in range(2):
        lo = (2 + sp) * rows
        base = sp * tall
        at = sum(EARLY) + sp * (cols // LANES) * HALO_W
        side_at = sum(EARLY) + 2 * (cols // LANES) * HALO_W
        extend(
            ext,
            base + HALO_W,
            base + HALO_W + rows,
            tile_ref[lo : lo + rows, :],
            strip_ref[lo : lo + rows, :],
        )
        for ref, start, flag in (
            (top_ref, base, s_at > 0),
            (bot_ref, base + HALO_W + rows, s_at < lax.axis_size("sx") - 1),
        ):
            parts = [
                masked(flag, ref[at + i * HALO_W : at + (i + 1) * HALO_W, :])
                for i in range(cols // LANES)
            ]
            sides = masked(flag, ref[side_at : side_at + SUB, :])
            strips = []
            for i in range(HALO_W // SUB):
                n = sp * (HALO_W // SUB) + i
                strips.append(
                    jnp.where(
                        lax.axis_index("sy") == 0,
                        pltpu.roll(sides, (LANES - n * SIDE) % LANES, 1),
                        pltpu.roll(sides, (2 * LANES - (n + 1) * SIDE) % LANES, 1),
                    )
                )
            extend(
                ext,
                start,
                start + HALO_W,
                jnp.concatenate(parts, axis=1),
                jnp.concatenate(strips, axis=0),
            )
    for d in range(count):
        outs[d][...] = packed(window(ext, 0, 2 * tall, wide * (me ^ d)))


def interleave_body(count, *refs):
    cens, (coef_ref, mid, down_ref, up_ref) = refs[:count], refs[count:]
    edge_rows((down_ref, up_ref), coef_ref, len(EARLY), LATE, (count - 1) * 2 * HALO)
    rows = cens[0].shape[0] // 2
    me = lax.axis_index("tm")
    for d in range(count):
        slab = me ^ d
        g, j = slab // PER_GROUP, slab % PER_GROUP
        for sp in range(2):
            mid[g, pl.ds(sp * PER_GROUP + j, rows, stride=SUB), :] = cens[d][
                sp * rows : (sp + 1) * rows, :
            ]

        @pl.when(slab < count - 1)
        def _(d=d, slab=slab):
            for sp in range(2):
                at = pl.multiple_of((slab * 2 + sp) * HALO, SUB)
                down_ref[pl.ds(at, HALO), :] = cens[d][(sp + 1) * rows - HALO : (sp + 1) * rows, :]
                up_ref[pl.ds(at, HALO), :] = cens[d][sp * rows : sp * rows + HALO, :]


def blocks(lo, hi):
    return [(r, min(r + BLOCK, hi)) for r in range(lo, hi, BLOCK)]


def shift(value, by):
    n = value.shape[0] // SUB
    return pltpu.roll(value.reshape(n, SUB, LANES), by, 1).reshape(n * SUB, LANES)


def at_rows(ref, lo, hi):
    return ref[lo * SUB : hi * SUB, :]


def masked(flag, value):
    return jnp.where(flag, value, jnp.zeros_like(value))


def each_group(groups, fn):
    if groups == 1:
        fn(0)
    else:
        lax.fori_loop(0, groups, lambda g, c: (fn(g), c)[1], 0)


def through_groups(groups, fn, carry):
    if groups == 1:
        fn(0, carry)
    else:
        lax.fori_loop(0, groups, fn, carry)


def slab_of(a, b):
    return lax.broadcasted_iota(jnp.int32, ((b - a) * SUB, LANES), 0) % PER_GROUP


def step(src, dst, lo, hi, coefs, seen=None):
    cv, ce, cd, cx = coefs[:4]
    for a, b in blocks(lo, hi):
        n = (b - a) * SUB
        rows = at_rows(src, a - 1, b + 1)
        face = at_rows(cv, a, b + 1)
        u = rows[SUB : SUB + n]
        e = at_rows(ce, a, b)
        east = pltpu.roll(u, LANES - 1, 1)
        new = at_rows(cd, a, b) * u + face[:n] * rows[:n] + face[SUB:] * rows[2 * SUB :]
        if len(coefs) > 4:
            new = new + at_rows(coefs[4], a, b)
        new = new + (e * east + pltpu.roll(e * u, 1, 1))
        new = new + at_rows(cx, a, b) * shift(u, PER_GROUP)
        dst[a * SUB : b * SUB, :] = new
        if seen is not None:
            seen(a, b, rows[:n], u, east, new)


def sweep(groups, one, two, lo, hi, coefs):
    def turn(t, carry):
        def run(g):
            step(one.at[g], two.at[g], lo, hi, coefs)
            step(two.at[g], one.at[g], lo, hi, coefs)

        each_group(groups, run)
        return carry

    lax.fori_loop(0, STEPS // 2, turn, 0)


def coarse(gd, cx, value, a, b):
    return at_rows(gd, a, b) * value + (STEPS * at_rows(cx, a, b)) * shift(value, PER_GROUP)


def load(groups, refs, tile_rows, mid, top_ref, bot_ref):
    s_at = lax.axis_index("sx")
    has_top = s_at > 0
    has_bot = s_at < lax.axis_size("sx") - 1
    end = HALO + tile_rows
    for g in range(groups):
        for ref in refs:
            ref[g, HALO * SUB : end * SUB, :] = mid[g]
        for j in range(PER_GROUP):
            for sp in range(2):
                slab = min(g * PER_GROUP + j, groups * PER_GROUP - 2)
                at = (slab * 2 + sp) * HALO
                for halo, start, flag in ((top_ref, 0, has_top), (bot_ref, end, has_bot)):
                    value = masked(flag, halo[at : at + HALO, :])
                    for ref in refs:
                        first = start * SUB + sp * PER_GROUP + j
                        ref[g, pl.ds(first, HALO, stride=SUB), :] = value


def spread(ref, sp, value):
    for j in range(PER_GROUP):
        ref[pl.ds(sp * PER_GROUP + j, value.shape[0], stride=SUB), :] = value


def coef_body(count, tile_rows, wide, coef_ref, top_ref, bot_ref, *rest):
    cv, ce, cd, gd, react_ref, flat = rest
    total = tile_rows + 2 * HALO
    k, rate = joined_rows(flat, coef_ref, (top_ref, bot_ref), 0, EARLY, 0)
    row = lax.broadcasted_iota(jnp.int32, (total, LANES), 0) + (
        lax.axis_index("sx") * tile_rows - HALO
    )
    col = lax.broadcasted_iota(jnp.int32, (total, LANES), 1) + (
        lax.axis_index("sy") * (wide * count) + lax.axis_index("tm") * wide - SIDE
    )
    all_rows = tile_rows * lax.axis_size("sx")
    all_cols = wide * count * lax.axis_size("sy")
    half = 0.5 * TIME_STEP
    above = half * (k + pltpu.roll(k, 1, 0))
    below = half * (k + pltpu.roll(k, total - 1, 0))
    east = half * (k + pltpu.roll(k, LANES - 1, 1))
    west = half * (k + pltpu.roll(k, 1, 1))
    faces = above + below + east + west
    above = jnp.where((row >= 1) & (row < all_rows), above, 0.0)
    east = jnp.where((col >= 0) & (col < all_cols - 1), east, 0.0)
    react = TIME_STEP * rate
    react_ref[...] = react
    for sp in range(2):
        spread(cv, sp, DIFFUSION[sp] * above)
        spread(ce, sp, DIFFUSION[sp] * east)
        spread(cd, sp, 1.0 - DIFFUSION[sp] * faces - DECAY[sp] * react)
        spread(gd, sp, 1.0 - (DECAY[sp] * STEPS) * react)


def state_body(
    count,
    tile_rows,
    mid,
    top_ref,
    bot_ref,
    coef_ref,
    cv,
    ce,
    cd,
    gd,
    react_ref,
    hist,
    slope,
    last_ref,
    cx,
    *rest,
):
    guess, one, two, cq, tg, flat = rest
    groups = count // PER_GROUP
    total = tile_rows + 2 * HALO
    coefs = (cv, ce, cd, cx, cq)
    coupling, *sources = joined_rows(
        flat, coef_ref, (top_ref, bot_ref), len(EARLY), LATE, (count - 1) * 2 * HALO
    )
    cross = react_ref[...] * coupling
    for sp in range(2):
        spread(cx, sp, cross)
        spread(cq, sp, TIME_STEP * sources[sp])
        spread(tg, sp, sources[2 + sp])
    lo, hi = STEPS, total - STEPS
    load(groups, (guess, one), tile_rows, mid, top_ref, bot_ref)
    sweep(groups, one, two, 1, total - 1, coefs)
    for a, b in blocks(lo, hi):
        slab = slab_of(a, b)

        def chain(g, carry, a=a, b=b, slab=slab):
            x = at_rows(one.at[g], a, b) - coarse(gd, cx, at_rows(guess.at[g], a, b), a, b)
            value = carry
            for _ in range(PER_GROUP - 1):
                value = jnp.where(
                    slab == 0, carry, shift(coarse(gd, cx, value, a, b) + x, 1)
                )
            two[g, a * SUB : b * SUB, :] = value
            return shift(coarse(gd, cx, value, a, b) + x, SUB - PER_GROUP + 1)

        through_groups(groups, chain, jnp.zeros(((b - a) * SUB, LANES), jnp.float32))

    def forward(turn, carry):
        def run(g):
            for k, (src, dst) in enumerate(((two, one), (one, two))):
                t = 2 * turn + k

                def seen(a, b, before, here, east, new, t=t):
                    hist[t, g, (a - lo) * SUB : (b - lo) * SUB, :] = here
                    if HALO <= a < HALO + tile_rows:
                        at = slice((a - HALO) * SUB, (b - HALO) * SUB)
                        slope[t, g, at, :] = east - here

                step(src.at[g], dst.at[g], lo, hi, coefs, seen)

        each_group(groups, run)
        return carry

    lax.fori_loop(0, STEPS // 2, forward, 0)
    w_lo, w_hi = 2 * STEPS, total - 2 * STEPS
    last_ref[...] = at_rows(two.at[groups - 1], w_lo, w_hi) - at_rows(tg, w_lo, w_hi)


def lag_body(count, tile_rows, *refs):
    cens, (cv, ce, cd, cx, gd, lag, guess, one, two) = refs[:count], refs[count:]
    groups = count // PER_GROUP
    total = tile_rows + 2 * HALO
    tall = tile_rows + 2 * HALO_W
    me = lax.axis_index("tm")
    for d in range(count):
        slab = me ^ d
        g, j = slab // PER_GROUP, slab % PER_GROUP
        both = unpacked(cens[d][...])
        for sp in range(2):
            start = (HALO - HALO_W) * SUB + sp * PER_GROUP + j
            value = both[sp * tall : (sp + 1) * tall, :]
            guess[g, pl.ds(start, tall, stride=SUB), :] = value
            one[g, pl.ds(start, tall, stride=SUB), :] = value
    sweep(groups, one, two, STEPS + 1, total - STEPS - 1, (cv, ce, cd, cx))
    w_lo, w_hi = 2 * STEPS, total - 2 * STEPS

    def run(g):
        for a, b in blocks(w_lo, w_hi):
            lag[g, (a - w_lo) * SUB : (b - w_lo) * SUB, :] = at_rows(
                one.at[g], a, b
            ) - coarse(gd, cx, at_rows(guess.at[g], a, b), a, b)

    each_group(groups, run)


def adjoint_body(count, tile_rows, lag, hist, slope, last_ref, cv, ce, cd, cx, gd, *rest):
    outs = rest[:count]
    one, two, fv, fh = rest[count:]
    groups = count // PER_GROUP
    total = tile_rows + 2 * HALO
    end = HALO + tile_rows
    coefs = (cv, ce, cd, cx)
    lo = STEPS
    me = lax.axis_index("tm")
    w_lo, w_hi = 2 * STEPS, total - 2 * STEPS
    for a, b in blocks(w_lo, w_hi):
        slab = slab_of(a, b)

        def chain(turn, carry, a=a, b=b, slab=slab):
            g = groups - 1 - turn
            y = lag[g, (a - w_lo) * SUB : (b - w_lo) * SUB, :]
            top = jnp.where(slab == PER_GROUP - 1, carry, 0.0)
            value = top
            for _ in range(PER_GROUP - 1):
                value = jnp.where(
                    slab == PER_GROUP - 1,
                    top,
                    shift(coarse(gd, cx, value, a, b) + y, SUB - 1),
                )
            two[g, a * SUB : b * SUB, :] = value
            return shift(coarse(gd, cx, value, a, b) + y, PER_GROUP - 1)

        through_groups(groups, chain, at_rows(last_ref, a - w_lo, b - w_lo))

    def clear(g):
        for r in (w_lo - 1, w_hi):
            for ref in (one, two):
                ref[g, r * SUB : (r + 1) * SUB, :] = jnp.zeros((SUB, LANES), jnp.float32)

    each_group(groups, clear)

    lane = lax.broadcasted_iota(jnp.int32, (tile_rows, LANES), 1)
    left = lane < LANES // 2

    def paired(first, second):
        return jnp.where(
            left,
            pltpu.roll(first, LANES - SIDE, 1),
            pltpu.roll(second, LANES // 2 - SIDE, 1),
        )

    for d in range(count):
        slab = me ^ d
        g, j = slab // PER_GROUP, slab % PER_GROUP
        s_rows = [
            hist[0, g, pl.ds((HALO - lo) * SUB + sp * PER_GROUP + j, tile_rows, stride=SUB), :]
            for sp in range(2)
        ]
        w_rows = [
            two[g, pl.ds(HALO * SUB + sp * PER_GROUP + j, tile_rows, stride=SUB), :]
            for sp in range(2)
        ]
        outs[d][0:tile_rows, :] = paired(*s_rows)
        outs[d][tile_rows : 2 * tile_rows, :] = paired(*w_rows)

    fv[...] = jnp.zeros_like(fv)
    fh[...] = jnp.zeros_like(fh)

    def products(t, g, a, b, before, here, east):
        if a < HALO or a > end:
            return
        at = slice((a - HALO) * SUB, (b - HALO) * SUB)
        u = hist[t, g, (a - lo - 1) * SUB : (b - lo) * SUB, :]
        fv[at, :] += (u[SUB:] - u[:-SUB]) * (here - before)
        if b <= end:
            fh[at, :] += slope[t, g, at, :] * (east - here)

    def back_step(src, dst, t, g):
        step(
            src.at[g],
            dst.at[g],
            w_lo,
            w_hi,
            coefs,
            lambda a, b, before, here, east, new: products(t, g, a, b, before, here, east),
        )

    def back(turn, carry):
        t = STEPS - 1 - 2 * turn

        def run(g):
            back_step(two, one, t, g)
            back_step(one, two, t - 1, g)

        each_group(groups, run)
        return carry

    lax.fori_loop(0, STEPS // 2 - 1, back, 0)

    def finish(g):
        back_step(two, one, 1, g)
        for a, b in blocks(HALO, end + BLOCK):
            rows = at_rows(one.at[g], a - 1, b)
            here = rows[SUB:]
            east = pltpu.roll(here, LANES - 1, 1) if b <= end else None
            products(0, g, a, b, rows[:-SUB], here, east)

    each_group(groups, finish)

    size = tile_rows * SUB
    fh[...] = fv[0:size, :] + fv[SUB : size + SUB, :] + fh[...] + pltpu.roll(fh[...], 1, 1)
    summed = []
    for sp in range(2):
        parts = [
            fh[pl.ds(sp * PER_GROUP + j, tile_rows, stride=SUB), :] for j in range(PER_GROUP)
        ]
        summed.append((parts[0] + parts[1]) + (parts[2] + parts[3]))
    gradient = (-0.5 * TIME_STEP) * (DIFFUSION[0] * summed[0] + DIFFUSION[1] * summed[1])
    middle = tile_rows // 2
    fold = jnp.where(
        left[:middle],
        pltpu.roll(gradient[:middle], LANES - SIDE, 1),
        pltpu.roll(gradient[middle:], LANES // 2 - SIDE, 1),
    )
    for d in range(count):
        outs[d][2 * tile_rows :, :] = fold


def collect_body(count, wide, *refs):
    parts = refs[:count]
    s_ref, w_ref, g_ref, held = refs[count:]
    me = lax.axis_index("tm")
    for d in range(count):
        held[me ^ d] = parts[d][...]
    rows = g_ref.shape[0]
    middle = rows // 2
    per = LANES // wide
    lane = lax.broadcasted_iota(jnp.int32, (rows, LANES), 1)

    def joined(lo, hi, start, v):
        value = None
        for i in range(per):
            t = v * per + i
            piece = held[t, lo:hi, :]
            turn = (i * wide - start) % LANES
            if turn:
                piece = pltpu.roll(piece, turn, 1)
            value = piece if i == 0 else jnp.where(lane[: hi - lo] >= i * wide, piece, value)
        return value

    for v in range(count // per):
        at = slice(v * LANES, (v + 1) * LANES)
        for sp in range(2):
            start = sp * (LANES // 2)
            s_ref[sp * rows : (sp + 1) * rows, at] = joined(0, rows, start, v)
            w_ref[sp * rows : (sp + 1) * rows, at] = joined(rows, 2 * rows, start, v)
            g_ref[sp * middle : (sp + 1) * middle, at] = joined(
                2 * rows, 2 * rows + middle, start, v
            )


def local(state_guess, adjoint_guess, diffusivity, decay_rate, coupling, control, target):
    rows, cols = diffusivity.shape
    count = lax.axis_size("tm")
    groups = count // PER_GROUP
    wide = cols // count
    total = rows + 2 * HALO
    fields = (
        state_guess.reshape(2 * rows, cols),
        adjoint_guess.reshape(2 * rows, cols),
        diffusivity,
        decay_rate,
        coupling,
        control.reshape(2 * rows, cols),
        target.reshape(2 * rows, cols),
    )

    def exchanged(parts):
        return [parts[0]] + [
            lax.ppermute(parts[d], "tm", [(i, i ^ d) for i in range(count)])
            for d in range(1, count)
        ]

    def turned(down, up):
        n = lax.axis_size("sx")
        return (
            lax.ppermute(down, "sx", [(i, (i + 1) % n) for i in range(n)]),
            lax.ppermute(up, "sx", [((i + 1) % n, i) for i in range(n)]),
        )

    tile, strip = call(
        fetch_body,
        [(11 * rows, cols), (11 * rows, LANES)],
        [pltpu.SemaphoreType.DMA((7,))],
        inputs=[HBM_SPEC] * 7,
    )(*[pltpu.with_memory_space_constraint(f, pltpu.HBM) for f in fields])
    strip = lax.ppermute(strip, "sy", [(0, 1), (1, 0)])
    edge = (sum(EARLY) + 2 * (cols // LANES) * HALO_W + SUB, LANES)
    windows = call(
        functools.partial(window_body, count, rows),
        [(2 * rows, LANES)] * count,
        [pltpu.VMEM((2 * rows, cols + 2 * LANES), jnp.float32)],
    )(tile, strip)
    states = exchanged(windows)
    coef, down, up = call(
        functools.partial(edge_body, count, rows),
        [(7 * rows, LANES), edge, edge],
        [pltpu.VMEM((7 * rows, cols + 2 * LANES), jnp.float32)],
    )(tile, strip, windows[0])
    edges = turned(down, up)
    mid, down, up = call(
        functools.partial(interleave_body, count),
        [(groups, rows * SUB, LANES)] + [((count - 1) * 2 * HALO + sum(LATE), LANES)] * 2,
    )(*states, coef)
    state_edges = turned(down, up)
    tall = rows + 2 * HALO_W
    windows = call(
        functools.partial(adjoint_window_body, count, rows),
        [(2 * tall * 3 // 4, LANES)] * count,
        [pltpu.VMEM((2 * tall, cols + 2 * LANES), jnp.float32)],
    )(tile, strip, *edges, mid)
    adjoints = exchanged(windows)
    plain = (total * SUB, LANES)
    work = pltpu.VMEM((groups, total * SUB, LANES), jnp.float32)
    limit = 60 << 20 if groups > 1 else 32 << 20
    cv, ce, cd, gd, react = call(
        functools.partial(coef_body, count, rows, wide),
        [plain] * 4 + [(total, LANES)],
        [pltpu.VMEM((len(EARLY), total, LANES), jnp.float32)],
    )(coef, *edges)
    hist, slope, last, cx = call(
        functools.partial(state_body, count, rows),
        [
            (STEPS, groups, (total - 2 * STEPS) * SUB, LANES),
            (STEPS, groups, rows * SUB, LANES),
            ((total - 4 * STEPS) * SUB, LANES),
            plain,
        ],
        [
            *([work] * 3),
            *([pltpu.VMEM(plain, jnp.float32)] * 2),
            pltpu.VMEM((len(LATE), total, LANES), jnp.float32),
        ],
        limit,
    )(mid, *state_edges, coef, cv, ce, cd, gd, react)
    (lag,) = call(
        functools.partial(lag_body, count, rows),
        [(groups, (total - 4 * STEPS) * SUB, LANES)],
        [work] * 3,
        limit,
    )(*adjoints, cv, ce, cd, cx, gd)
    outs = call(
        functools.partial(adjoint_body, count, rows),
        [(2 * rows + rows // 2, LANES)] * count,
        [
            *([work] * 2),
            pltpu.VMEM(((rows + BLOCK) * SUB, LANES), jnp.float32),
            pltpu.VMEM((rows * SUB, LANES), jnp.float32),
        ],
        limit,
    )(lag, hist, slope, last, cv, ce, cd, cx, gd)
    outs = exchanged(outs)
    states, adjoints, gradient = call(
        functools.partial(collect_body, count, wide),
        [(2 * rows, cols), (2 * rows, cols), (rows, cols)],
        [pltpu.VMEM((count, 2 * rows + rows // 2, LANES), jnp.float32)],
    )(*outs)
    return (
        states.reshape(1, 2, rows, cols),
        adjoints.reshape(1, 2, rows, cols),
        gradient,
    )


def solution(mesh):
    placed = (
        P("tm", None, "sx", "sy"),
        P("tm", None, "sx", "sy"),
        P("sx", "sy"),
        P("sx", "sy"),
        P("sx", "sy"),
        P(None, "sx", "sy"),
        P(None, "sx", "sy"),
    )
    return jax.shard_map(
        local,
        mesh=mesh,
        in_specs=placed,
        out_specs=(P("tm", None, "sx", "sy"), P("tm", None, "sx", "sy"), P("sx", "sy")),
        check_vma=False,
    )
```

```python
import functools

import jax
import jax.numpy as jnp
from jax import lax
from jax.experimental import pallas as pl
from jax.experimental.pallas import tpu as pltpu
from jax.sharding import PartitionSpec as P

STEPS = 8
TIME_STEP = 0.1
DIFFUSION = (1.0, 0.4)
DECAY = (1.0, 2.0)

LANES = 128
SUB = 8
PER_GROUP = 4
HALO = 3 * STEPS
HALO_W = 2 * STEPS
SIDE = 32
BLOCK = 8
PARTS = (0, STEPS // 2)
TURNS = STEPS // (2 * len(PARTS))

VMEM_SPEC = pl.BlockSpec(memory_space=pltpu.VMEM)
HBM_SPEC = pl.BlockSpec(memory_space=pltpu.HBM)


def call(body, outs, scratch=(), limit=32 << 20, inputs=None, aliases=None):
    def run(*args):
        return pl.pallas_call(
            body,
            out_shape=[jax.ShapeDtypeStruct(s, jnp.float32) for s in outs],
            in_specs=inputs or [VMEM_SPEC] * len(args),
            out_specs=[VMEM_SPEC] * len(outs),
            scratch_shapes=list(scratch),
            input_output_aliases=aliases or {},
            compiler_params=pltpu.CompilerParams(vmem_limit_bytes=limit),
        )(*args)

    return run


def fetch_body(*refs):
    fields, (tile_ref, strip_ref, sems) = refs[:7], refs[7:]
    cols = tile_ref.shape[1]
    copies = []
    at = 0
    for i, ref in enumerate(fields):
        rows = ref.shape[0]
        copies.append(
            pltpu.make_async_copy(ref, tile_ref.at[at : at + rows, :], sems.at[i])
        )
        at += rows
    for copy in copies:
        copy.start()
    for copy in copies:
        copy.wait()
    strip_ref[...] = jnp.where(
        lax.axis_index("sy") == 0, tile_ref[:, cols - LANES :], tile_ref[:, :LANES]
    )


EARLY = (HALO,) * 2
LATE = (HALO,) * 3 + (SUB,) * 2


def edge_rows(refs, coef_ref, first, sizes, at):
    down_ref, up_ref = refs
    rows = coef_ref.shape[0] // 7
    for f, size in enumerate(sizes, first):
        down_ref[at : at + size, :] = coef_ref[(f + 1) * rows - size : (f + 1) * rows, :]
        up_ref[at : at + size, :] = coef_ref[f * rows : f * rows + size, :]
        at += size
    return at


def joined_rows(flat, coef_ref, refs, first, sizes, at):
    s_at = lax.axis_index("sx")
    has_top = s_at > 0
    has_bot = s_at < lax.axis_size("sx") - 1
    top_ref, bot_ref = refs
    rows = coef_ref.shape[0] // 7
    end = HALO + rows
    fields = []
    for i, size in enumerate(sizes):
        f = first + i
        flat[i, HALO - size : HALO, :] = masked(has_top, top_ref[at : at + size, :])
        flat[i, HALO:end, :] = coef_ref[f * rows : (f + 1) * rows, :]
        flat[i, end : end + size, :] = masked(has_bot, bot_ref[at : at + size, :])
        fields.append(flat[i])
        at += size
    return fields


def extend(ext, lo, hi, tile, strip):
    first = lax.axis_index("sy") == 0
    cols = tile.shape[1]
    zero = jnp.zeros_like(strip)
    ext[lo:hi, 0:LANES] = jnp.where(first, zero, strip)
    ext[lo:hi, LANES : LANES + cols] = tile
    ext[lo:hi, LANES + cols : 2 * LANES + cols] = jnp.where(first, strip, zero)


def window(ext, lo, hi, start):
    start = start + LANES - SIDE
    base = pl.multiple_of((start // LANES) * LANES, LANES)
    turn = 2 * LANES - start % LANES
    return pltpu.roll(ext[lo:hi, pl.ds(base, 2 * LANES)], turn, 1)[:, :LANES]


PACKED = 3 * LANES // 4


def packed(value):
    n = value.shape[0] // 4
    cut = (LANES - PACKED) // 2
    lane = lax.broadcasted_iota(jnp.int32, (n, LANES), 1)
    last = value[3 * n :]
    parts = []
    for i in range(3):
        main = pltpu.roll(value[i * n : (i + 1) * n], LANES - cut, 1)
        rest = pltpu.roll(last, (PACKED - cut - i * (LANES - PACKED)) % LANES, 1)
        parts.append(jnp.where(lane < PACKED, main, rest))
    return jnp.concatenate(parts, axis=0)


def unpacked(value):
    n = value.shape[0] // 3
    cut = (LANES - PACKED) // 2
    side = LANES - PACKED
    lane = lax.broadcasted_iota(jnp.int32, (n, LANES), 1)
    parts, last = [], None
    for i in range(3):
        part = value[i * n : (i + 1) * n]
        parts.append(pltpu.roll(part, cut, 1))
        rest = pltpu.roll(part, (cut + i * side - PACKED) % LANES, 1)
        last = rest if i == 0 else jnp.where(lane >= cut + i * side, rest, last)
    return jnp.concatenate([*parts, last], axis=0)


def window_body(count, rows, tile_ref, strip_ref, *refs):
    outs, ext = refs[:count], refs[count]
    me = lax.axis_index("tm")
    wide = tile_ref.shape[1] // count
    extend(ext, 0, 2 * rows, tile_ref[: 2 * rows, :], strip_ref[: 2 * rows, :])
    for d in range(count):
        outs[d][...] = window(ext, 0, 2 * rows, wide * (me ^ d))


def edge_body(count, rows, tile_ref, strip_ref, after, *refs):
    del after
    outs, (coef_ref, down_ref, up_ref, ext) = refs[:count], refs[count:]
    me = lax.axis_index("tm")
    cols = tile_ref.shape[1]
    wide = cols // count
    extend(ext, 0, 9 * rows, tile_ref[2 * rows :, :], strip_ref[2 * rows :, :])
    coef_ref[...] = window(ext, 2 * rows, 9 * rows, wide * me)
    for d in range(count):
        outs[d][: 2 * rows * PACKED // LANES, :] = packed(
            window(ext, 0, 2 * rows, wide * (me ^ d))
        )
    at = edge_rows((down_ref, up_ref), coef_ref, 0, EARLY, 0)
    lane = lax.broadcasted_iota(jnp.int32, (SUB, LANES), 1)
    for ref, low in ((down_ref, rows - HALO_W), (up_ref, 0)):
        put, sides = at, None
        for sp in range(2):
            here = (2 + sp) * rows + low
            for i in range(cols // LANES):
                ref[put : put + HALO_W, :] = tile_ref[
                    here : here + HALO_W, i * LANES : (i + 1) * LANES
                ]
                put += HALO_W
            for i in range(HALO_W // SUB):
                strip = strip_ref[here + i * SUB : here + (i + 1) * SUB, :]
                n = sp * (HALO_W // SUB) + i
                strip = jnp.where(
                    lax.axis_index("sy") == 0,
                    pltpu.roll(strip, n * SIDE, 1),
                    pltpu.roll(strip, (n + 1) * SIDE % LANES, 1),
                )
                sides = strip if n == 0 else jnp.where(lane >= n * SIDE, strip, sides)
        ref[put : put + SUB, :] = sides


def adjoint_window_body(count, rows, cols, top_ref, bot_ref, after, *refs):
    del after
    outs, ext = refs[count : 2 * count], refs[2 * count]
    me = lax.axis_index("tm")
    s_at = lax.axis_index("sx")
    wide = cols // count
    for sp in range(2):
        base = sp * 2 * HALO_W
        at = sum(EARLY) + sp * (cols // LANES) * HALO_W
        side_at = sum(EARLY) + 2 * (cols // LANES) * HALO_W
        for ref, start, flag in (
            (top_ref, base, s_at > 0),
            (bot_ref, base + HALO_W, s_at < lax.axis_size("sx") - 1),
        ):
            parts = [
                masked(flag, ref[at + i * HALO_W : at + (i + 1) * HALO_W, :])
                for i in range(cols // LANES)
            ]
            sides = masked(flag, ref[side_at : side_at + SUB, :])
            strips = []
            for i in range(HALO_W // SUB):
                n = sp * (HALO_W // SUB) + i
                strips.append(
                    jnp.where(
                        lax.axis_index("sy") == 0,
                        pltpu.roll(sides, (LANES - n * SIDE) % LANES, 1),
                        pltpu.roll(sides, (2 * LANES - (n + 1) * SIDE) % LANES, 1),
                    )
                )
            extend(
                ext,
                start,
                start + HALO_W,
                jnp.concatenate(parts, axis=1),
                jnp.concatenate(strips, axis=0),
            )
    for d in range(count):
        outs[d][2 * rows * PACKED // LANES :, :] = packed(
            window(ext, 0, 4 * HALO_W, wide * (me ^ d))
        )


def interleave_body(count, *refs):
    cens, (coef_ref, mid, down_ref, up_ref) = refs[:count], refs[count:]
    edge_rows((down_ref, up_ref), coef_ref, len(EARLY), LATE, (count - 1) * 2 * HALO)
    rows = cens[0].shape[0] // 2
    me = lax.axis_index("tm")
    for d in range(count):
        slab = me ^ (-d % count)
        g, j = slab // PER_GROUP, slab % PER_GROUP
        for sp in range(2):
            mid[g, pl.ds(sp * PER_GROUP + j, rows, stride=SUB), :] = cens[d][
                sp * rows : (sp + 1) * rows, :
            ]

        @pl.when(slab < count - 1)
        def _(d=d, slab=slab):
            for sp in range(2):
                at = pl.multiple_of((slab * 2 + sp) * HALO, SUB)
                down_ref[pl.ds(at, HALO), :] = cens[d][(sp + 1) * rows - HALO : (sp + 1) * rows, :]
                up_ref[pl.ds(at, HALO), :] = cens[d][sp * rows : sp * rows + HALO, :]


def blocks(lo, hi):
    return [(r, min(r + BLOCK, hi)) for r in range(lo, hi, BLOCK)]


def shift(value, by):
    n = value.shape[0] // SUB
    return pltpu.roll(value.reshape(n, SUB, LANES), by, 1).reshape(n * SUB, LANES)


def at_rows(ref, lo, hi):
    return ref[lo * SUB : hi * SUB, :]


def masked(flag, value):
    return jnp.where(flag, value, jnp.zeros_like(value))


def each_group(groups, fn):
    if groups == 1:
        fn(0)
    else:
        lax.fori_loop(0, groups, lambda g, c: (fn(g), c)[1], 0)


def through_groups(groups, fn, carry):
    if groups == 1:
        fn(0, carry)
    else:
        lax.fori_loop(0, groups, fn, carry)


def slab_of(a, b):
    return lax.broadcasted_iota(jnp.int32, ((b - a) * SUB, LANES), 0) % PER_GROUP


def step(src, dst, lo, hi, coefs, seen=None):
    cv, ce, cd, cx = coefs[:4]
    for a, b in blocks(lo, hi):
        n = (b - a) * SUB
        rows = at_rows(src, a - 1, b + 1)
        face = at_rows(cv, a, b + 1)
        u = rows[SUB : SUB + n]
        e = at_rows(ce, a, b)
        east = pltpu.roll(u, LANES - 1, 1)
        new = at_rows(cd, a, b) * u + face[:n] * rows[:n] + face[SUB:] * rows[2 * SUB :]
        if len(coefs) > 4:
            new = new + at_rows(coefs[4], a, b)
        new = new + (e * east + pltpu.roll(e * u, 1, 1))
        new = new + at_rows(cx, a, b) * shift(u, PER_GROUP)
        dst[a * SUB : b * SUB, :] = new
        if seen is not None:
            seen(a, b, rows[:n], u, east, new)


def sweep(groups, one, two, lo, hi, coefs):
    for cut in PARTS:

        def turn(t, carry, a=lo + cut, b=hi - cut):
            def run(g):
                step(one.at[g], two.at[g], a, b, coefs)
                step(two.at[g], one.at[g], a, b, coefs)

            each_group(groups, run)
            return carry

        lax.fori_loop(0, TURNS, turn, 0)


def coarse(gd, cx, value, a, b):
    return at_rows(gd, a, b) * value + (STEPS * at_rows(cx, a, b)) * shift(value, PER_GROUP)


def load(groups, refs, tile_rows, mid, top_ref, bot_ref):
    s_at = lax.axis_index("sx")
    has_top = s_at > 0
    has_bot = s_at < lax.axis_size("sx") - 1
    end = HALO + tile_rows
    for g in range(groups):
        for ref in refs:
            ref[g, HALO * SUB : end * SUB, :] = mid[g]
        for j in range(PER_GROUP):
            for sp in range(2):
                slab = min(g * PER_GROUP + j, groups * PER_GROUP - 2)
                at = (slab * 2 + sp) * HALO
                for halo, start, flag in ((top_ref, 0, has_top), (bot_ref, end, has_bot)):
                    value = masked(flag, halo[at : at + HALO, :])
                    for ref in refs:
                        first = start * SUB + sp * PER_GROUP + j
                        ref[g, pl.ds(first, HALO, stride=SUB), :] = value


def spread(ref, sp, value):
    for j in range(PER_GROUP):
        ref[pl.ds(sp * PER_GROUP + j, value.shape[0], stride=SUB), :] = value


def coef_body(count, tile_rows, wide, coef_ref, top_ref, bot_ref, *rest):
    cv, ce, cd, gd, react_ref, flat = rest
    total = tile_rows + 2 * HALO
    k, rate = joined_rows(flat, coef_ref, (top_ref, bot_ref), 0, EARLY, 0)
    row = lax.broadcasted_iota(jnp.int32, (total, LANES), 0) + (
        lax.axis_index("sx") * tile_rows - HALO
    )
    col = lax.broadcasted_iota(jnp.int32, (total, LANES), 1) + (
        lax.axis_index("sy") * (wide * count) + lax.axis_index("tm") * wide - SIDE
    )
    all_rows = tile_rows * lax.axis_size("sx")
    all_cols = wide * count * lax.axis_size("sy")
    half = 0.5 * TIME_STEP
    above = half * (k + pltpu.roll(k, 1, 0))
    below = half * (k + pltpu.roll(k, total - 1, 0))
    east = half * (k + pltpu.roll(k, LANES - 1, 1))
    west = half * (k + pltpu.roll(k, 1, 1))
    faces = above + below + east + west
    above = jnp.where((row >= 1) & (row < all_rows), above, 0.0)
    east = jnp.where((col >= 0) & (col < all_cols - 1), east, 0.0)
    react = TIME_STEP * rate
    react_ref[...] = react
    for sp in range(2):
        spread(cv, sp, DIFFUSION[sp] * above)
        spread(ce, sp, DIFFUSION[sp] * east)
        spread(cd, sp, 1.0 - DIFFUSION[sp] * faces - DECAY[sp] * react)
        spread(gd, sp, 1.0 - (DECAY[sp] * STEPS) * react)


def state_body(
    count,
    tile_rows,
    mid,
    top_ref,
    bot_ref,
    coef_ref,
    cv,
    ce,
    cd,
    gd,
    react_ref,
    hist,
    slope,
    last_ref,
    cx,
    *rest,
):
    guess, one, two, cq, tg, flat = rest
    groups = count // PER_GROUP
    total = tile_rows + 2 * HALO
    coefs = (cv, ce, cd, cx, cq)
    coupling, *sources = joined_rows(
        flat, coef_ref, (top_ref, bot_ref), len(EARLY), LATE, (count - 1) * 2 * HALO
    )
    cross = react_ref[...] * coupling
    for sp in range(2):
        spread(cx, sp, cross)
        spread(cq, sp, TIME_STEP * sources[sp])
        spread(tg, sp, sources[2 + sp])
    lo, hi = STEPS, total - STEPS
    load(groups, (guess, one), tile_rows, mid, top_ref, bot_ref)
    sweep(groups, one, two, 1, total - 1, coefs)
    for a, b in blocks(lo, hi):
        slab = slab_of(a, b)

        def chain(g, carry, a=a, b=b, slab=slab):
            x = at_rows(one.at[g], a, b) - coarse(gd, cx, at_rows(guess.at[g], a, b), a, b)
            value = carry
            for _ in range(PER_GROUP - 1):
                value = jnp.where(
                    slab == 0, carry, shift(coarse(gd, cx, value, a, b) + x, 1)
                )
            two[g, a * SUB : b * SUB, :] = value
            return shift(coarse(gd, cx, value, a, b) + x, SUB - PER_GROUP + 1)

        through_groups(groups, chain, jnp.zeros(((b - a) * SUB, LANES), jnp.float32))

    for i, cut in enumerate(PARTS):

        def forward(turn, carry, base=2 * TURNS * i, cut=cut):
            def run(g):
                for k, (src, dst) in enumerate(((two, one), (one, two))):
                    t = base + 2 * turn + k

                    def seen(a, b, before, here, east, new, t=t):
                        hist[t, g, (a - lo) * SUB : (b - lo) * SUB, :] = here
                        p, q = max(a, HALO), min(b, HALO + tile_rows)
                        if p < q:
                            rise = (east - here)[(p - a) * SUB : (q - a) * SUB]
                            slope[t, g, (p - HALO) * SUB : (q - HALO) * SUB, :] = rise

                    step(src.at[g], dst.at[g], lo + cut, hi - cut, coefs, seen)

            each_group(groups, run)
            return carry

        lax.fori_loop(0, TURNS, forward, 0)
    w_lo, w_hi = 2 * STEPS, total - 2 * STEPS
    last_ref[...] = at_rows(two.at[groups - 1], w_lo, w_hi) - at_rows(tg, w_lo, w_hi)


def lag_body(count, tile_rows, *refs):
    cens, (cv, ce, cd, cx, gd, lag, guess, one, two) = refs[:count], refs[count:]
    groups = count // PER_GROUP
    total = tile_rows + 2 * HALO
    me = lax.axis_index("tm")
    for d in range(count):
        slab = me ^ d
        g, j = slab // PER_GROUP, slab % PER_GROUP
        split = 2 * tile_rows * PACKED // LANES
        inner, outer = unpacked(cens[d][:split, :]), unpacked(cens[d][split:, :])
        for sp in range(2):
            edge = 2 * HALO_W * sp
            for start, value in (
                (HALO, inner[sp * tile_rows : (sp + 1) * tile_rows]),
                (HALO - HALO_W, outer[edge : edge + HALO_W]),
                (HALO + tile_rows, outer[edge + HALO_W : edge + 2 * HALO_W]),
            ):
                at = pl.ds(start * SUB + sp * PER_GROUP + j, value.shape[0], stride=SUB)
                guess[g, at, :] = value
                one[g, at, :] = value
    sweep(groups, one, two, STEPS + 1, total - STEPS - 1, (cv, ce, cd, cx))
    w_lo, w_hi = 2 * STEPS, total - 2 * STEPS

    def run(g):
        for a, b in blocks(w_lo, w_hi):
            lag[g, (a - w_lo) * SUB : (b - w_lo) * SUB, :] = at_rows(
                one.at[g], a, b
            ) - coarse(gd, cx, at_rows(guess.at[g], a, b), a, b)

    each_group(groups, run)


def adjoint_body(count, tile_rows, lag, hist, slope, last_ref, cv, ce, cd, cx, gd, *rest):
    outs = rest[:count]
    one, two, fv, fh = rest[count:]
    groups = count // PER_GROUP
    total = tile_rows + 2 * HALO
    end = HALO + tile_rows
    coefs = (cv, ce, cd, cx)
    lo = STEPS
    me = lax.axis_index("tm")
    w_lo, w_hi = 2 * STEPS, total - 2 * STEPS
    for a, b in blocks(w_lo, w_hi):
        slab = slab_of(a, b)

        def chain(turn, carry, a=a, b=b, slab=slab):
            g = groups - 1 - turn
            y = lag[g, (a - w_lo) * SUB : (b - w_lo) * SUB, :]
            top = jnp.where(slab == PER_GROUP - 1, carry, 0.0)
            value = top
            for _ in range(PER_GROUP - 1):
                value = jnp.where(
                    slab == PER_GROUP - 1,
                    top,
                    shift(coarse(gd, cx, value, a, b) + y, SUB - 1),
                )
            two[g, a * SUB : b * SUB, :] = value
            return shift(coarse(gd, cx, value, a, b) + y, PER_GROUP - 1)

        through_groups(groups, chain, at_rows(last_ref, a - w_lo, b - w_lo))

    def clear(g):
        for r in (w_lo - 1, w_hi):
            for ref in (one, two):
                ref[g, r * SUB : (r + 1) * SUB, :] = jnp.zeros((SUB, LANES), jnp.float32)

    each_group(groups, clear)

    lane = lax.broadcasted_iota(jnp.int32, (tile_rows, LANES), 1)
    left = lane < LANES // 2

    def paired(first, second):
        return jnp.where(
            left,
            pltpu.roll(first, LANES - SIDE, 1),
            pltpu.roll(second, LANES // 2 - SIDE, 1),
        )

    for d in range(count):
        slab = me ^ d
        g, j = slab // PER_GROUP, slab % PER_GROUP
        s_rows = [
            hist[0, g, pl.ds((HALO - lo) * SUB + sp * PER_GROUP + j, tile_rows, stride=SUB), :]
            for sp in range(2)
        ]
        w_rows = [
            two[g, pl.ds(HALO * SUB + sp * PER_GROUP + j, tile_rows, stride=SUB), :]
            for sp in range(2)
        ]
        outs[d][0:tile_rows, :] = paired(*s_rows)
        outs[d][tile_rows : 2 * tile_rows, :] = paired(*w_rows)

    fv[...] = jnp.zeros_like(fv)
    fh[...] = jnp.zeros_like(fh)

    def products(t, g, a, b, before, here, east):
        for ref, stop in ((fv, end + 1), (fh, end)):
            p, q = max(a, HALO), min(b, stop)
            if p >= q:
                continue
            at = slice((p - HALO) * SUB, (q - HALO) * SUB)
            part = slice((p - a) * SUB, (q - a) * SUB)
            if ref is fv:
                u = hist[t, g, (p - lo - 1) * SUB : (q - lo) * SUB, :]
                ref[at, :] += (u[SUB:] - u[:-SUB]) * (here[part] - before[part])
            else:
                ref[at, :] += slope[t, g, at, :] * (east[part] - here[part])

    def back_step(src, dst, t, g, cut):
        step(
            src.at[g],
            dst.at[g],
            w_lo + cut,
            w_hi - cut,
            coefs,
            lambda a, b, before, here, east, new: products(t, g, a, b, before, here, east),
        )

    def back(turn, carry):
        t = STEPS - 1 - 2 * turn

        def run(g):
            back_step(two, one, t, g, 0)
            back_step(one, two, t - 1, g, 0)

        each_group(groups, run)
        return carry

    lax.fori_loop(0, TURNS, back, 0)

    def finish(g):
        cut = 2 * TURNS
        for t in range(STEPS - 1 - cut, 0, -1):
            src, dst = (two, one) if t % 2 else (one, two)
            back_step(src, dst, t, g, cut)
        for a, b in blocks(HALO, end + 1):
            rows = at_rows(one.at[g], a - 1, b)
            here = rows[SUB:]
            products(0, g, a, b, rows[:-SUB], here, pltpu.roll(here, LANES - 1, 1))

    each_group(groups, finish)

    size = tile_rows * SUB
    fh[...] = fv[0:size, :] + fv[SUB : size + SUB, :] + fh[...] + pltpu.roll(fh[...], 1, 1)
    summed = []
    for sp in range(2):
        parts = [
            fh[pl.ds(sp * PER_GROUP + j, tile_rows, stride=SUB), :] for j in range(PER_GROUP)
        ]
        summed.append((parts[0] + parts[1]) + (parts[2] + parts[3]))
    gradient = (-0.5 * TIME_STEP) * (DIFFUSION[0] * summed[0] + DIFFUSION[1] * summed[1])
    middle = tile_rows // 2
    fold = jnp.where(
        left[:middle],
        pltpu.roll(gradient[:middle], LANES - SIDE, 1),
        pltpu.roll(gradient[middle:], LANES // 2 - SIDE, 1),
    )
    for d in range(count):
        outs[d][2 * tile_rows :, :] = fold


def collect_body(count, wide, *refs):
    parts = refs[:count]
    s_ref, w_ref, g_ref, held = refs[count:]
    me = lax.axis_index("tm")
    for d in range(count):
        held[me ^ (-d % count)] = parts[d][...]
    rows = g_ref.shape[0]
    middle = rows // 2
    per = LANES // wide
    lane = lax.broadcasted_iota(jnp.int32, (rows, LANES), 1)

    def joined(lo, hi, start, v):
        value = None
        for i in range(per):
            t = v * per + i
            piece = held[t, lo:hi, :]
            turn = (i * wide - start) % LANES
            if turn:
                piece = pltpu.roll(piece, turn, 1)
            value = piece if i == 0 else jnp.where(lane[: hi - lo] >= i * wide, piece, value)
        return value

    for v in range(count // per):
        at = slice(v * LANES, (v + 1) * LANES)
        for sp in range(2):
            start = sp * (LANES // 2)
            s_ref[sp * rows : (sp + 1) * rows, at] = joined(0, rows, start, v)
            w_ref[sp * rows : (sp + 1) * rows, at] = joined(rows, 2 * rows, start, v)
            g_ref[sp * middle : (sp + 1) * middle, at] = joined(
                2 * rows, 2 * rows + middle, start, v
            )


def local(state_guess, adjoint_guess, diffusivity, decay_rate, coupling, control, target):
    rows, cols = diffusivity.shape
    count = lax.axis_size("tm")
    groups = count // PER_GROUP
    wide = cols // count
    total = rows + 2 * HALO
    fields = (
        state_guess.reshape(2 * rows, cols),
        adjoint_guess.reshape(2 * rows, cols),
        diffusivity,
        decay_rate,
        coupling,
        control.reshape(2 * rows, cols),
        target.reshape(2 * rows, cols),
    )

    def exchanged(parts, far_first=True):
        order = range(count - 1, 0, -1) if far_first else range(1, count)
        return [parts[0]] + [
            lax.ppermute(parts[d], "tm", [(i, i ^ d) for i in range(count)]) for d in order
        ]

    def turned(down, up):
        n = lax.axis_size("sx")
        return (
            lax.ppermute(down, "sx", [(i, (i + 1) % n) for i in range(n)]),
            lax.ppermute(up, "sx", [((i + 1) % n, i) for i in range(n)]),
        )

    tile, strip = call(
        fetch_body,
        [(11 * rows, cols), (11 * rows, LANES)],
        [pltpu.SemaphoreType.DMA((7,))],
        inputs=[HBM_SPEC] * 7,
    )(*[pltpu.with_memory_space_constraint(f, pltpu.HBM) for f in fields])
    strip = lax.ppermute(strip, "sy", [(0, 1), (1, 0)])
    edge = (sum(EARLY) + 2 * (cols // LANES) * HALO_W + SUB, LANES)
    windows = call(
        functools.partial(window_body, count, rows),
        [(2 * rows, LANES)] * count,
        [pltpu.VMEM((2 * rows, cols + 2 * LANES), jnp.float32)],
    )(tile, strip)
    states = exchanged(windows)
    size = 2 * (rows + 2 * HALO_W) * PACKED // LANES
    *inner, coef, down, up = call(
        functools.partial(edge_body, count, rows),
        [(size, LANES)] * count + [(7 * rows, LANES), edge, edge],
        [pltpu.VMEM((9 * rows, cols + 2 * LANES), jnp.float32)],
    )(tile, strip, windows[0])
    edges = turned(down, up)
    mid, down, up = call(
        functools.partial(interleave_body, count),
        [(groups, rows * SUB, LANES)] + [((count - 1) * 2 * HALO + sum(LATE), LANES)] * 2,
    )(*states, coef)
    state_edges = turned(down, up)
    windows = call(
        functools.partial(adjoint_window_body, count, rows, cols),
        [(size, LANES)] * count,
        [pltpu.VMEM((4 * HALO_W, cols + 2 * LANES), jnp.float32)],
        aliases={3 + d: d for d in range(count)},
    )(*edges, mid, *inner)
    adjoints = exchanged(windows, far_first=False)
    plain = (total * SUB, LANES)
    work = pltpu.VMEM((groups, total * SUB, LANES), jnp.float32)
    limit = 60 << 20 if groups > 1 else 32 << 20
    cv, ce, cd, gd, react = call(
        functools.partial(coef_body, count, rows, wide),
        [plain] * 4 + [(total, LANES)],
        [pltpu.VMEM((len(EARLY), total, LANES), jnp.float32)],
    )(coef, *edges)
    hist, slope, last, cx = call(
        functools.partial(state_body, count, rows),
        [
            (STEPS, groups, (total - 2 * STEPS) * SUB, LANES),
            (STEPS, groups, rows * SUB, LANES),
            ((total - 4 * STEPS) * SUB, LANES),
            plain,
        ],
        [
            *([work] * 3),
            *([pltpu.VMEM(plain, jnp.float32)] * 2),
            pltpu.VMEM((len(LATE), total, LANES), jnp.float32),
        ],
        limit,
    )(mid, *state_edges, coef, cv, ce, cd, gd, react)
    (lag,) = call(
        functools.partial(lag_body, count, rows),
        [(groups, (total - 4 * STEPS) * SUB, LANES)],
        [work] * 3,
        limit,
    )(*adjoints, cv, ce, cd, cx, gd)
    outs = call(
        functools.partial(adjoint_body, count, rows),
        [(2 * rows + rows // 2, LANES)] * count,
        [
            *([work] * 2),
            pltpu.VMEM(((rows + 1) * SUB, LANES), jnp.float32),
            pltpu.VMEM((rows * SUB, LANES), jnp.float32),
        ],
        limit,
    )(lag, hist, slope, last, cv, ce, cd, cx, gd)
    outs = exchanged(outs)
    states, adjoints, gradient = call(
        functools.partial(collect_body, count, wide),
        [(2 * rows, cols), (2 * rows, cols), (rows, cols)],
        [pltpu.VMEM((count, 2 * rows + rows // 2, LANES), jnp.float32)],
    )(*outs)
    return (
        states.reshape(1, 2, rows, cols),
        adjoints.reshape(1, 2, rows, cols),
        gradient,
    )


def solution(mesh):
    placed = (
        P("tm", None, "sx", "sy"),
        P("tm", None, "sx", "sy"),
        P("sx", "sy"),
        P("sx", "sy"),
        P("sx", "sy"),
        P(None, "sx", "sy"),
        P(None, "sx", "sy"),
    )
    return jax.shard_map(
        local,
        mesh=mesh,
        in_specs=placed,
        out_specs=(P("tm", None, "sx", "sy"), P("tm", None, "sx", "sy"), P("sx", "sy")),
        check_vma=False,
    )
```

```python
import functools

import jax
import jax.numpy as jnp
from jax import lax
from jax.experimental import pallas as pl
from jax.experimental.pallas import tpu as pltpu
from jax.sharding import PartitionSpec as P

STEPS = 8
TIME_STEP = 0.1
DIFFUSION = (1.0, 0.4)
DECAY = (1.0, 2.0)

LANES = 128
SUB = 8
PER_GROUP = 4
HALO = 3 * STEPS
HALO_W = 2 * STEPS
SIDE = 32
BLOCK = 8
PARTS = (0, STEPS // 2)
TURNS = STEPS // (2 * len(PARTS))

VMEM_SPEC = pl.BlockSpec(memory_space=pltpu.VMEM)
HBM_SPEC = pl.BlockSpec(memory_space=pltpu.HBM)


def call(body, outs, scratch=(), limit=32 << 20, inputs=None, aliases=None):
    def run(*args):
        return pl.pallas_call(
            body,
            out_shape=[jax.ShapeDtypeStruct(s, jnp.float32) for s in outs],
            in_specs=inputs or [VMEM_SPEC] * len(args),
            out_specs=[VMEM_SPEC] * len(outs),
            scratch_shapes=list(scratch),
            input_output_aliases=aliases or {},
            compiler_params=pltpu.CompilerParams(vmem_limit_bytes=limit),
        )(*args)

    return run


def copied(copies):
    for copy in copies:
        copy.start()
    for copy in copies:
        copy.wait()


def strip_body(*refs):
    fields, (strip_ref, sems) = refs[:7], refs[7:]
    cols = fields[0].shape[1]
    start = pl.multiple_of(
        jnp.where(lax.axis_index("sy") == 0, cols - LANES, 0).astype(jnp.int32), LANES
    )
    copies = []
    at = 0
    for i, ref in enumerate(fields):
        rows = ref.shape[0]
        copies.append(
            pltpu.make_async_copy(
                ref.at[:, pl.ds(start, LANES)], strip_ref.at[at : at + rows, :], sems.at[i]
            )
        )
        at += rows
    copied(copies)


def tile_body(*refs):
    fields, (after, tile_ref, sems) = refs[:7], refs[7:]
    del after
    copies = []
    at = 0
    for i, ref in enumerate(fields):
        rows = ref.shape[0]
        copies.append(
            pltpu.make_async_copy(ref, tile_ref.at[at : at + rows, :], sems.at[i])
        )
        at += rows
    copied(copies)


EARLY = (HALO,) * 2
LATE = (HALO,) * 3 + (SUB,) * 2


def even_row():
    return lax.axis_index("sx") % 2 == 0


def send_rows(refs, at, down, up):
    refs[0][at, :] = jnp.where(even_row(), down, up)
    refs[1][at, :] = jnp.where(even_row(), up, down)


def received(refs, lo, hi):
    s_at = lax.axis_index("sx")
    first, second = refs[0][lo:hi, :], refs[1][lo:hi, :]
    top = jnp.where(even_row(), second, first)
    bot = jnp.where(even_row(), first, second)
    return masked(s_at > 0, top), masked(s_at < lax.axis_size("sx") - 1, bot)


def edge_rows(refs, coef_ref, first, sizes, at):
    rows = coef_ref.shape[0] // 7
    for f, size in enumerate(sizes, first):
        send_rows(
            refs,
            slice(at, at + size),
            coef_ref[(f + 1) * rows - size : (f + 1) * rows, :],
            coef_ref[f * rows : f * rows + size, :],
        )
        at += size
    return at


def joined_rows(flat, coef_ref, refs, first, sizes, at):
    rows = coef_ref.shape[0] // 7
    end = HALO + rows
    fields = []
    for i, size in enumerate(sizes):
        f = first + i
        top, bot = received(refs, at, at + size)
        flat[i, HALO - size : HALO, :] = top
        flat[i, HALO:end, :] = coef_ref[f * rows : (f + 1) * rows, :]
        flat[i, end : end + size, :] = bot
        fields.append(flat[i])
        at += size
    return fields


def extend(ext, lo, hi, tile, strip):
    first = lax.axis_index("sy") == 0
    cols = tile.shape[1]
    zero = jnp.zeros_like(strip)
    ext[lo:hi, 0:LANES] = jnp.where(first, zero, strip)
    ext[lo:hi, LANES : LANES + cols] = tile
    ext[lo:hi, LANES + cols : 2 * LANES + cols] = jnp.where(first, strip, zero)


def window(ext, lo, hi, start):
    start = start + LANES - SIDE
    base = pl.multiple_of((start // LANES) * LANES, LANES)
    turn = 2 * LANES - start % LANES
    return pltpu.roll(ext[lo:hi, pl.ds(base, 2 * LANES)], turn, 1)[:, :LANES]


PACKED = 3 * LANES // 4


def packed(value):
    n = value.shape[0] // 4
    cut = (LANES - PACKED) // 2
    lane = lax.broadcasted_iota(jnp.int32, (n, LANES), 1)
    last = value[3 * n :]
    parts = []
    for i in range(3):
        main = pltpu.roll(value[i * n : (i + 1) * n], LANES - cut, 1)
        rest = pltpu.roll(last, (PACKED - cut - i * (LANES - PACKED)) % LANES, 1)
        parts.append(jnp.where(lane < PACKED, main, rest))
    return jnp.concatenate(parts, axis=0)


def unpacked(value):
    n = value.shape[0] // 3
    cut = (LANES - PACKED) // 2
    side = LANES - PACKED
    lane = lax.broadcasted_iota(jnp.int32, (n, LANES), 1)
    parts, last = [], None
    for i in range(3):
        part = value[i * n : (i + 1) * n]
        parts.append(pltpu.roll(part, cut, 1))
        rest = pltpu.roll(part, (cut + i * side - PACKED) % LANES, 1)
        last = rest if i == 0 else jnp.where(lane >= cut + i * side, rest, last)
    return jnp.concatenate([*parts, last], axis=0)


def window_body(count, rows, tile_ref, strip_ref, *refs):
    outs, ext = refs[:count], refs[count]
    me = lax.axis_index("tm")
    wide = tile_ref.shape[1] // count
    extend(ext, 0, 2 * rows, tile_ref[: 2 * rows, :], strip_ref[: 2 * rows, :])
    for d in range(count):
        outs[d][...] = window(ext, 0, 2 * rows, wide * (me ^ d))


def edge_body(count, rows, tile_ref, strip_ref, after, *refs):
    del after
    outs, (coef_ref, down_ref, up_ref, ext) = refs[:count], refs[count:]
    me = lax.axis_index("tm")
    cols = tile_ref.shape[1]
    wide = cols // count
    extend(ext, 0, 9 * rows, tile_ref[2 * rows :, :], strip_ref[2 * rows :, :])
    coef_ref[...] = window(ext, 2 * rows, 9 * rows, wide * me)
    for d in range(count):
        outs[d][: 2 * rows * PACKED // LANES, :] = packed(
            window(ext, 0, 2 * rows, wide * (me ^ d))
        )
    at = edge_rows((down_ref, up_ref), coef_ref, 0, EARLY, 0)
    lane = lax.broadcasted_iota(jnp.int32, (SUB, LANES), 1)
    sides = [None, None]
    for sp in range(2):
        lo = (2 + sp) * rows
        starts = (lo + rows - HALO_W, lo)
        for i in range(cols // LANES):
            send_rows(
                (down_ref, up_ref),
                slice(at, at + HALO_W),
                *[tile_ref[p : p + HALO_W, i * LANES : (i + 1) * LANES] for p in starts],
            )
            at += HALO_W
        for i in range(HALO_W // SUB):
            n = sp * (HALO_W // SUB) + i
            for side, p in enumerate(starts):
                strip = strip_ref[p + i * SUB : p + (i + 1) * SUB, :]
                strip = jnp.where(
                    lax.axis_index("sy") == 0,
                    pltpu.roll(strip, n * SIDE, 1),
                    pltpu.roll(strip, (n + 1) * SIDE % LANES, 1),
                )
                sides[side] = (
                    strip if n == 0 else jnp.where(lane >= n * SIDE, strip, sides[side])
                )
    send_rows((down_ref, up_ref), slice(at, at + SUB), *sides)


def adjoint_window_body(count, rows, cols, top_ref, bot_ref, after, *refs):
    del after
    outs, ext = refs[count : 2 * count], refs[2 * count]
    me = lax.axis_index("tm")
    wide = cols // count
    for sp in range(2):
        base = sp * 2 * HALO_W
        at = sum(EARLY) + sp * (cols // LANES) * HALO_W
        side_at = sum(EARLY) + 2 * (cols // LANES) * HALO_W
        pieces = [
            received((top_ref, bot_ref), at + i * HALO_W, at + (i + 1) * HALO_W)
            for i in range(cols // LANES)
        ]
        both = received((top_ref, bot_ref), side_at, side_at + SUB)
        for side, start in enumerate((base, base + HALO_W)):
            parts = [piece[side] for piece in pieces]
            sides = both[side]
            strips = []
            for i in range(HALO_W // SUB):
                n = sp * (HALO_W // SUB) + i
                strips.append(
                    jnp.where(
                        lax.axis_index("sy") == 0,
                        pltpu.roll(sides, (LANES - n * SIDE) % LANES, 1),
                        pltpu.roll(sides, (2 * LANES - (n + 1) * SIDE) % LANES, 1),
                    )
                )
            extend(
                ext,
                start,
                start + HALO_W,
                jnp.concatenate(parts, axis=1),
                jnp.concatenate(strips, axis=0),
            )
    for d in range(count):
        outs[d][2 * rows * PACKED // LANES :, :] = packed(
            window(ext, 0, 4 * HALO_W, wide * (me ^ d))
        )


def interleave_body(count, *refs):
    cens, (coef_ref, mid, down_ref, up_ref) = refs[:count], refs[count:]
    edge_rows((down_ref, up_ref), coef_ref, len(EARLY), LATE, (count - 1) * 2 * HALO)
    rows = cens[0].shape[0] // 2
    me = lax.axis_index("tm")
    for d in range(count):
        slab = me ^ (-d % count)
        g, j = slab // PER_GROUP, slab % PER_GROUP
        for sp in range(2):
            mid[g, pl.ds(sp * PER_GROUP + j, rows, stride=SUB), :] = cens[d][
                sp * rows : (sp + 1) * rows, :
            ]

        @pl.when(slab < count - 1)
        def _(d=d, slab=slab):
            for sp in range(2):
                at = pl.multiple_of((slab * 2 + sp) * HALO, SUB)
                send_rows(
                    (down_ref, up_ref),
                    pl.ds(at, HALO),
                    cens[d][(sp + 1) * rows - HALO : (sp + 1) * rows, :],
                    cens[d][sp * rows : sp * rows + HALO, :],
                )


def blocks(lo, hi):
    return [(r, min(r + BLOCK, hi)) for r in range(lo, hi, BLOCK)]


def shift(value, by):
    n = value.shape[0] // SUB
    return pltpu.roll(value.reshape(n, SUB, LANES), by, 1).reshape(n * SUB, LANES)


def at_rows(ref, lo, hi):
    return ref[lo * SUB : hi * SUB, :]


def masked(flag, value):
    return jnp.where(flag, value, jnp.zeros_like(value))


def each_group(groups, fn):
    if groups == 1:
        fn(0)
    else:
        lax.fori_loop(0, groups, lambda g, c: (fn(g), c)[1], 0)


def through_groups(groups, fn, carry):
    if groups == 1:
        fn(0, carry)
    else:
        lax.fori_loop(0, groups, fn, carry)


def slab_of(a, b):
    return lax.broadcasted_iota(jnp.int32, ((b - a) * SUB, LANES), 0) % PER_GROUP


def step(src, dst, lo, hi, coefs, seen=None):
    cv, ce, cd, cx = coefs[:4]
    for a, b in blocks(lo, hi):
        n = (b - a) * SUB
        rows = at_rows(src, a - 1, b + 1)
        face = at_rows(cv, a, b + 1)
        u = rows[SUB : SUB + n]
        e = at_rows(ce, a, b)
        east = pltpu.roll(u, LANES - 1, 1)
        new = at_rows(cd, a, b) * u + face[:n] * rows[:n] + face[SUB:] * rows[2 * SUB :]
        if len(coefs) > 4:
            new = new + at_rows(coefs[4], a, b)
        new = new + (e * east + pltpu.roll(e * u, 1, 1))
        new = new + at_rows(cx, a, b) * shift(u, PER_GROUP)
        dst[a * SUB : b * SUB, :] = new
        if seen is not None:
            seen(a, b, rows[:n], u, east, new)


def sweep(groups, one, two, lo, hi, coefs):
    for cut in PARTS:

        def turn(t, carry, a=lo + cut, b=hi - cut):
            def run(g):
                step(one.at[g], two.at[g], a, b, coefs)
                step(two.at[g], one.at[g], a, b, coefs)

            each_group(groups, run)
            return carry

        lax.fori_loop(0, TURNS, turn, 0)


def coarse(gd, cx, value, a, b):
    return at_rows(gd, a, b) * value + (STEPS * at_rows(cx, a, b)) * shift(value, PER_GROUP)


def load(groups, refs, tile_rows, mid, top_ref, bot_ref):
    end = HALO + tile_rows
    for g in range(groups):
        for ref in refs:
            ref[g, HALO * SUB : end * SUB, :] = mid[g]
        for j in range(PER_GROUP):
            for sp in range(2):
                slab = min(g * PER_GROUP + j, groups * PER_GROUP - 2)
                at = (slab * 2 + sp) * HALO
                values = received((top_ref, bot_ref), at, at + HALO)
                for value, start in zip(values, (0, end)):
                    for ref in refs:
                        first = start * SUB + sp * PER_GROUP + j
                        ref[g, pl.ds(first, HALO, stride=SUB), :] = value


def spread(ref, sp, value):
    for j in range(PER_GROUP):
        ref[pl.ds(sp * PER_GROUP + j, value.shape[0], stride=SUB), :] = value


def coef_body(count, tile_rows, wide, coef_ref, top_ref, bot_ref, *rest):
    cv, ce, cd, gd, react_ref, flat = rest
    total = tile_rows + 2 * HALO
    k, rate = joined_rows(flat, coef_ref, (top_ref, bot_ref), 0, EARLY, 0)
    row = lax.broadcasted_iota(jnp.int32, (total, LANES), 0) + (
        lax.axis_index("sx") * tile_rows - HALO
    )
    col = lax.broadcasted_iota(jnp.int32, (total, LANES), 1) + (
        lax.axis_index("sy") * (wide * count) + lax.axis_index("tm") * wide - SIDE
    )
    all_rows = tile_rows * lax.axis_size("sx")
    all_cols = wide * count * lax.axis_size("sy")
    half = 0.5 * TIME_STEP
    above = half * (k + pltpu.roll(k, 1, 0))
    below = half * (k + pltpu.roll(k, total - 1, 0))
    east = half * (k + pltpu.roll(k, LANES - 1, 1))
    west = half * (k + pltpu.roll(k, 1, 1))
    faces = above + below + east + west
    above = jnp.where((row >= 1) & (row < all_rows), above, 0.0)
    east = jnp.where((col >= 0) & (col < all_cols - 1), east, 0.0)
    react = TIME_STEP * rate
    react_ref[...] = react
    for sp in range(2):
        spread(cv, sp, DIFFUSION[sp] * above)
        spread(ce, sp, DIFFUSION[sp] * east)
        spread(cd, sp, 1.0 - DIFFUSION[sp] * faces - DECAY[sp] * react)
        spread(gd, sp, 1.0 - (DECAY[sp] * STEPS) * react)


def state_body(
    count,
    tile_rows,
    mid,
    top_ref,
    bot_ref,
    coef_ref,
    cv,
    ce,
    cd,
    gd,
    react_ref,
    hist,
    slope,
    last_ref,
    cx,
    *rest,
):
    guess, one, two, cq, tg, flat = rest
    groups = count // PER_GROUP
    total = tile_rows + 2 * HALO
    coefs = (cv, ce, cd, cx, cq)
    coupling, *sources = joined_rows(
        flat, coef_ref, (top_ref, bot_ref), len(EARLY), LATE, (count - 1) * 2 * HALO
    )
    cross = react_ref[...] * coupling
    for sp in range(2):
        spread(cx, sp, cross)
        spread(cq, sp, TIME_STEP * sources[sp])
        spread(tg, sp, sources[2 + sp])
    lo, hi = STEPS, total - STEPS
    load(groups, (guess, one), tile_rows, mid, top_ref, bot_ref)
    sweep(groups, one, two, 1, total - 1, coefs)
    for a, b in blocks(lo, hi):
        slab = slab_of(a, b)

        def chain(g, carry, a=a, b=b, slab=slab):
            x = at_rows(one.at[g], a, b) - coarse(gd, cx, at_rows(guess.at[g], a, b), a, b)
            value = carry
            for _ in range(PER_GROUP - 1):
                value = jnp.where(
                    slab == 0, carry, shift(coarse(gd, cx, value, a, b) + x, 1)
                )
            two[g, a * SUB : b * SUB, :] = value
            return shift(coarse(gd, cx, value, a, b) + x, SUB - PER_GROUP + 1)

        through_groups(groups, chain, jnp.zeros(((b - a) * SUB, LANES), jnp.float32))

    for i, cut in enumerate(PARTS):

        def forward(turn, carry, base=2 * TURNS * i, cut=cut):
            def run(g):
                for k, (src, dst) in enumerate(((two, one), (one, two))):
                    t = base + 2 * turn + k

                    def seen(a, b, before, here, east, new, t=t):
                        hist[t, g, (a - lo) * SUB : (b - lo) * SUB, :] = here
                        p, q = max(a, HALO), min(b, HALO + tile_rows)
                        if p < q:
                            rise = (east - here)[(p - a) * SUB : (q - a) * SUB]
                            slope[t, g, (p - HALO) * SUB : (q - HALO) * SUB, :] = rise

                    step(src.at[g], dst.at[g], lo + cut, hi - cut, coefs, seen)

            each_group(groups, run)
            return carry

        lax.fori_loop(0, TURNS, forward, 0)
    w_lo, w_hi = 2 * STEPS, total - 2 * STEPS
    last_ref[...] = at_rows(two.at[groups - 1], w_lo, w_hi) - at_rows(tg, w_lo, w_hi)


def lag_body(count, tile_rows, *refs):
    cens, (cv, ce, cd, cx, gd, lag, guess, one, two) = refs[:count], refs[count:]
    groups = count // PER_GROUP
    total = tile_rows + 2 * HALO
    me = lax.axis_index("tm")
    for d in range(count):
        slab = me ^ d
        g, j = slab // PER_GROUP, slab % PER_GROUP
        split = 2 * tile_rows * PACKED // LANES
        inner, outer = unpacked(cens[d][:split, :]), unpacked(cens[d][split:, :])
        for sp in range(2):
            edge = 2 * HALO_W * sp
            for start, value in (
                (HALO, inner[sp * tile_rows : (sp + 1) * tile_rows]),
                (HALO - HALO_W, outer[edge : edge + HALO_W]),
                (HALO + tile_rows, outer[edge + HALO_W : edge + 2 * HALO_W]),
            ):
                at = pl.ds(start * SUB + sp * PER_GROUP + j, value.shape[0], stride=SUB)
                guess[g, at, :] = value
                one[g, at, :] = value
    sweep(groups, one, two, STEPS + 1, total - STEPS - 1, (cv, ce, cd, cx))
    w_lo, w_hi = 2 * STEPS, total - 2 * STEPS

    def run(g):
        for a, b in blocks(w_lo, w_hi):
            lag[g, (a - w_lo) * SUB : (b - w_lo) * SUB, :] = at_rows(
                one.at[g], a, b
            ) - coarse(gd, cx, at_rows(guess.at[g], a, b), a, b)

    each_group(groups, run)


def adjoint_body(count, tile_rows, lag, hist, slope, last_ref, cv, ce, cd, cx, gd, *rest):
    outs = rest[:count]
    one, two, fv, fh = rest[count:]
    groups = count // PER_GROUP
    total = tile_rows + 2 * HALO
    end = HALO + tile_rows
    coefs = (cv, ce, cd, cx)
    lo = STEPS
    me = lax.axis_index("tm")
    w_lo, w_hi = 2 * STEPS, total - 2 * STEPS
    for a, b in blocks(w_lo, w_hi):
        slab = slab_of(a, b)

        def chain(turn, carry, a=a, b=b, slab=slab):
            g = groups - 1 - turn
            y = lag[g, (a - w_lo) * SUB : (b - w_lo) * SUB, :]
            top = jnp.where(slab == PER_GROUP - 1, carry, 0.0)
            value = top
            for _ in range(PER_GROUP - 1):
                value = jnp.where(
                    slab == PER_GROUP - 1,
                    top,
                    shift(coarse(gd, cx, value, a, b) + y, SUB - 1),
                )
            two[g, a * SUB : b * SUB, :] = value
            return shift(coarse(gd, cx, value, a, b) + y, PER_GROUP - 1)

        through_groups(groups, chain, at_rows(last_ref, a - w_lo, b - w_lo))

    def clear(g):
        for r in (w_lo - 1, w_hi):
            for ref in (one, two):
                ref[g, r * SUB : (r + 1) * SUB, :] = jnp.zeros((SUB, LANES), jnp.float32)

    each_group(groups, clear)

    lane = lax.broadcasted_iota(jnp.int32, (tile_rows, LANES), 1)
    left = lane < LANES // 2

    def paired(first, second):
        return jnp.where(
            left,
            pltpu.roll(first, LANES - SIDE, 1),
            pltpu.roll(second, LANES // 2 - SIDE, 1),
        )

    for d in range(count):
        slab = me ^ d
        g, j = slab // PER_GROUP, slab % PER_GROUP
        s_rows = [
            hist[0, g, pl.ds((HALO - lo) * SUB + sp * PER_GROUP + j, tile_rows, stride=SUB), :]
            for sp in range(2)
        ]
        w_rows = [
            two[g, pl.ds(HALO * SUB + sp * PER_GROUP + j, tile_rows, stride=SUB), :]
            for sp in range(2)
        ]
        outs[d][0:tile_rows, :] = paired(*s_rows)
        outs[d][tile_rows : 2 * tile_rows, :] = paired(*w_rows)

    fv[...] = jnp.zeros_like(fv)
    fh[...] = jnp.zeros_like(fh)

    def products(t, g, a, b, before, here, east):
        for ref, stop in ((fv, end + 1), (fh, end)):
            p, q = max(a, HALO), min(b, stop)
            if p >= q:
                continue
            at = slice((p - HALO) * SUB, (q - HALO) * SUB)
            part = slice((p - a) * SUB, (q - a) * SUB)
            if ref is fv:
                u = hist[t, g, (p - lo - 1) * SUB : (q - lo) * SUB, :]
                ref[at, :] += (u[SUB:] - u[:-SUB]) * (here[part] - before[part])
            else:
                ref[at, :] += slope[t, g, at, :] * (east[part] - here[part])

    def back_step(src, dst, t, g, cut):
        step(
            src.at[g],
            dst.at[g],
            w_lo + cut,
            w_hi - cut,
            coefs,
            lambda a, b, before, here, east, new: products(t, g, a, b, before, here, east),
        )

    def back(turn, carry):
        t = STEPS - 1 - 2 * turn

        def run(g):
            back_step(two, one, t, g, 0)
            back_step(one, two, t - 1, g, 0)

        each_group(groups, run)
        return carry

    lax.fori_loop(0, TURNS, back, 0)

    def finish(g):
        cut = 2 * TURNS
        for t in range(STEPS - 1 - cut, 0, -1):
            src, dst = (two, one) if t % 2 else (one, two)
            back_step(src, dst, t, g, cut)
        for a, b in blocks(HALO, end + 1):
            rows = at_rows(one.at[g], a - 1, b)
            here = rows[SUB:]
            products(0, g, a, b, rows[:-SUB], here, pltpu.roll(here, LANES - 1, 1))

    each_group(groups, finish)

    size = tile_rows * SUB
    fh[...] = fv[0:size, :] + fv[SUB : size + SUB, :] + fh[...] + pltpu.roll(fh[...], 1, 1)
    summed = []
    for sp in range(2):
        parts = [
            fh[pl.ds(sp * PER_GROUP + j, tile_rows, stride=SUB), :] for j in range(PER_GROUP)
        ]
        summed.append((parts[0] + parts[1]) + (parts[2] + parts[3]))
    gradient = (-0.5 * TIME_STEP) * (DIFFUSION[0] * summed[0] + DIFFUSION[1] * summed[1])
    middle = tile_rows // 2
    fold = jnp.where(
        left[:middle],
        pltpu.roll(gradient[:middle], LANES - SIDE, 1),
        pltpu.roll(gradient[middle:], LANES // 2 - SIDE, 1),
    )
    for d in range(count):
        outs[d][2 * tile_rows :, :] = fold


def collect_body(count, wide, *refs):
    parts = refs[:count]
    s_ref, w_ref, g_ref, held = refs[count:]
    me = lax.axis_index("tm")
    for d in range(count):
        held[me ^ (-d % count)] = parts[d][...]
    rows = g_ref.shape[0]
    middle = rows // 2
    per = LANES // wide
    lane = lax.broadcasted_iota(jnp.int32, (rows, LANES), 1)

    def joined(lo, hi, start, v):
        value = None
        for i in range(per):
            t = v * per + i
            piece = held[t, lo:hi, :]
            turn = (i * wide - start) % LANES
            if turn:
                piece = pltpu.roll(piece, turn, 1)
            value = piece if i == 0 else jnp.where(lane[: hi - lo] >= i * wide, piece, value)
        return value

    for v in range(count // per):
        at = slice(v * LANES, (v + 1) * LANES)
        for sp in range(2):
            start = sp * (LANES // 2)
            s_ref[sp * rows : (sp + 1) * rows, at] = joined(0, rows, start, v)
            w_ref[sp * rows : (sp + 1) * rows, at] = joined(rows, 2 * rows, start, v)
            g_ref[sp * middle : (sp + 1) * middle, at] = joined(
                2 * rows, 2 * rows + middle, start, v
            )


def local(state_guess, adjoint_guess, diffusivity, decay_rate, coupling, control, target):
    rows, cols = diffusivity.shape
    count = lax.axis_size("tm")
    groups = count // PER_GROUP
    wide = cols // count
    total = rows + 2 * HALO
    fields = (
        state_guess.reshape(2 * rows, cols),
        adjoint_guess.reshape(2 * rows, cols),
        diffusivity,
        decay_rate,
        coupling,
        control.reshape(2 * rows, cols),
        target.reshape(2 * rows, cols),
    )

    def exchanged(parts, far_first=True):
        order = range(count - 1, 0, -1) if far_first else range(1, count)
        return [parts[0]] + [
            lax.ppermute(parts[d], "tm", [(i, i ^ d) for i in range(count)]) for d in order
        ]

    def turned(first, second):
        n = lax.axis_size("sx")
        return (
            lax.ppermute(first, "sx", [(i, i ^ 1) for i in range(n)]),
            lax.ppermute(second, "sx", [(i, (i + (1 if i % 2 else n - 1)) % n) for i in range(n)]),
        )

    fields = [pltpu.with_memory_space_constraint(f, pltpu.HBM) for f in fields]
    sems = [pltpu.SemaphoreType.DMA((7,))]
    (strip,) = call(strip_body, [(11 * rows, LANES)], sems, inputs=[HBM_SPEC] * 7)(*fields)
    (tile,) = call(tile_body, [(11 * rows, cols)], sems, inputs=[HBM_SPEC] * 7 + [VMEM_SPEC])(
        *fields, strip
    )
    strip = lax.ppermute(strip, "sy", [(0, 1), (1, 0)])
    edge = (sum(EARLY) + 2 * (cols // LANES) * HALO_W + SUB, LANES)
    windows = call(
        functools.partial(window_body, count, rows),
        [(2 * rows, LANES)] * count,
        [pltpu.VMEM((2 * rows, cols + 2 * LANES), jnp.float32)],
    )(tile, strip)
    states = exchanged(windows)
    size = 2 * (rows + 2 * HALO_W) * PACKED // LANES
    *inner, coef, down, up = call(
        functools.partial(edge_body, count, rows),
        [(size, LANES)] * count + [(7 * rows, LANES), edge, edge],
        [pltpu.VMEM((9 * rows, cols + 2 * LANES), jnp.float32)],
    )(tile, strip, windows[0])
    edges = turned(down, up)
    mid, down, up = call(
        functools.partial(interleave_body, count),
        [(groups, rows * SUB, LANES)] + [((count - 1) * 2 * HALO + sum(LATE), LANES)] * 2,
    )(*states, coef)
    state_edges = turned(down, up)
    windows = call(
        functools.partial(adjoint_window_body, count, rows, cols),
        [(size, LANES)] * count,
        [pltpu.VMEM((4 * HALO_W, cols + 2 * LANES), jnp.float32)],
        aliases={3 + d: d for d in range(count)},
    )(*edges, mid, *inner)
    adjoints = exchanged(windows, far_first=False)
    plain = (total * SUB, LANES)
    work = pltpu.VMEM((groups, total * SUB, LANES), jnp.float32)
    limit = 60 << 20 if groups > 1 else 32 << 20
    cv, ce, cd, gd, react = call(
        functools.partial(coef_body, count, rows, wide),
        [plain] * 4 + [(total, LANES)],
        [pltpu.VMEM((len(EARLY), total, LANES), jnp.float32)],
    )(coef, *edges)
    hist, slope, last, cx = call(
        functools.partial(state_body, count, rows),
        [
            (STEPS, groups, (total - 2 * STEPS) * SUB, LANES),
            (STEPS, groups, rows * SUB, LANES),
            ((total - 4 * STEPS) * SUB, LANES),
            plain,
        ],
        [
            *([work] * 3),
            *([pltpu.VMEM(plain, jnp.float32)] * 2),
            pltpu.VMEM((len(LATE), total, LANES), jnp.float32),
        ],
        limit,
    )(mid, *state_edges, coef, cv, ce, cd, gd, react)
    (lag,) = call(
        functools.partial(lag_body, count, rows),
        [(groups, (total - 4 * STEPS) * SUB, LANES)],
        [work] * 3,
        limit,
    )(*adjoints, cv, ce, cd, cx, gd)
    outs = call(
        functools.partial(adjoint_body, count, rows),
        [(2 * rows + rows // 2, LANES)] * count,
        [
            *([work] * 2),
            pltpu.VMEM(((rows + 1) * SUB, LANES), jnp.float32),
            pltpu.VMEM((rows * SUB, LANES), jnp.float32),
        ],
        limit,
    )(lag, hist, slope, last, cv, ce, cd, cx, gd)
    outs = exchanged(outs)
    states, adjoints, gradient = call(
        functools.partial(collect_body, count, wide),
        [(2 * rows, cols), (2 * rows, cols), (rows, cols)],
        [pltpu.VMEM((count, 2 * rows + rows // 2, LANES), jnp.float32)],
    )(*outs)
    return (
        states.reshape(1, 2, rows, cols),
        adjoints.reshape(1, 2, rows, cols),
        gradient,
    )


def solution(mesh):
    placed = (
        P("tm", None, "sx", "sy"),
        P("tm", None, "sx", "sy"),
        P("sx", "sy"),
        P("sx", "sy"),
        P("sx", "sy"),
        P(None, "sx", "sy"),
        P(None, "sx", "sy"),
    )
    return jax.shard_map(
        local,
        mesh=mesh,
        in_specs=placed,
        out_specs=(P("tm", None, "sx", "sy"), P("tm", None, "sx", "sy"), P("sx", "sy")),
        check_vma=False,
    )
```

```python
import functools

import jax
import jax.numpy as jnp
from jax import lax
from jax.experimental import pallas as pl
from jax.experimental.pallas import tpu as pltpu
from jax.sharding import PartitionSpec as P

STEPS = 8
TIME_STEP = 0.1
DIFFUSION = (1.0, 0.4)
DECAY = (1.0, 2.0)

LANES = 128
SUB = 8
PER_GROUP = 4
HALO = 3 * STEPS
HALO_W = 2 * STEPS
SIDE = 32
BLOCK = 8

VMEM_SPEC = pl.BlockSpec(memory_space=pltpu.VMEM)
HBM_SPEC = pl.BlockSpec(memory_space=pltpu.HBM)


def call(body, outs, scratch=(), limit=32 << 20, inputs=None, aliases=None):
    def run(*args):
        return pl.pallas_call(
            body,
            out_shape=[jax.ShapeDtypeStruct(s, jnp.float32) for s in outs],
            in_specs=inputs or [VMEM_SPEC] * len(args),
            out_specs=[VMEM_SPEC] * len(outs),
            scratch_shapes=list(scratch),
            input_output_aliases=aliases or {},
            compiler_params=pltpu.CompilerParams(vmem_limit_bytes=limit),
        )(*args)

    return run


def copied(copies):
    for copy in copies:
        copy.start()
    for copy in copies:
        copy.wait()


def strip_body(*refs):
    fields, (strip_ref, sems) = refs[:7], refs[7:]
    cols = fields[0].shape[1]
    start = pl.multiple_of(
        jnp.where(lax.axis_index("sy") == 0, cols - LANES, 0).astype(jnp.int32), LANES
    )
    copies = []
    at = 0
    for i, ref in enumerate(fields):
        rows = ref.shape[0]
        copies.append(
            pltpu.make_async_copy(
                ref.at[:, pl.ds(start, LANES)], strip_ref.at[at : at + rows, :], sems.at[i]
            )
        )
        at += rows
    copied(copies)


def tile_body(*refs):
    fields, (after, tile_ref, sems) = refs[:7], refs[7:]
    del after
    copies = []
    at = 0
    for i, ref in enumerate(fields):
        rows = ref.shape[0]
        copies.append(
            pltpu.make_async_copy(ref, tile_ref.at[at : at + rows, :], sems.at[i])
        )
        at += rows
    copied(copies)


EARLY = (HALO,) * 2
LATE = (HALO,) * 3 + (SUB,) * 2


def even_row():
    return lax.axis_index("sx") % 2 == 0


def send_rows(refs, at, down, up):
    refs[0][at, :] = jnp.where(even_row(), down, up)
    refs[1][at, :] = jnp.where(even_row(), up, down)


def received(refs, lo, hi):
    s_at = lax.axis_index("sx")
    first, second = refs[0][lo:hi, :], refs[1][lo:hi, :]
    top = jnp.where(even_row(), second, first)
    bot = jnp.where(even_row(), first, second)
    return masked(s_at > 0, top), masked(s_at < lax.axis_size("sx") - 1, bot)


def edge_rows(refs, coef_ref, first, sizes, at):
    rows = coef_ref.shape[0] // 7
    for f, size in enumerate(sizes, first):
        send_rows(
            refs,
            slice(at, at + size),
            coef_ref[(f + 1) * rows - size : (f + 1) * rows, :],
            coef_ref[f * rows : f * rows + size, :],
        )
        at += size
    return at


def joined_rows(flat, coef_ref, refs, first, sizes, at):
    rows = coef_ref.shape[0] // 7
    end = HALO + rows
    fields = []
    for i, size in enumerate(sizes):
        f = first + i
        top, bot = received(refs, at, at + size)
        flat[i, HALO - size : HALO, :] = top
        flat[i, HALO:end, :] = coef_ref[f * rows : (f + 1) * rows, :]
        flat[i, end : end + size, :] = bot
        fields.append(flat[i])
        at += size
    return fields


def extend(ext, lo, hi, tile, strip):
    first = lax.axis_index("sy") == 0
    cols = tile.shape[1]
    zero = jnp.zeros_like(strip)
    ext[lo:hi, 0:LANES] = jnp.where(first, zero, strip)
    ext[lo:hi, LANES : LANES + cols] = tile
    ext[lo:hi, LANES + cols : 2 * LANES + cols] = jnp.where(first, strip, zero)


def window(ext, lo, hi, start):
    start = start + LANES - SIDE
    base = pl.multiple_of((start // LANES) * LANES, LANES)
    turn = 2 * LANES - start % LANES
    return pltpu.roll(ext[lo:hi, pl.ds(base, 2 * LANES)], turn, 1)[:, :LANES]


PACKED = 3 * LANES // 4


def packed(value):
    n = value.shape[0] // 4
    cut = (LANES - PACKED) // 2
    lane = lax.broadcasted_iota(jnp.int32, (n, LANES), 1)
    last = value[3 * n :]
    parts = []
    for i in range(3):
        main = pltpu.roll(value[i * n : (i + 1) * n], LANES - cut, 1)
        rest = pltpu.roll(last, (PACKED - cut - i * (LANES - PACKED)) % LANES, 1)
        parts.append(jnp.where(lane < PACKED, main, rest))
    return jnp.concatenate(parts, axis=0)


def unpacked(value):
    n = value.shape[0] // 3
    cut = (LANES - PACKED) // 2
    side = LANES - PACKED
    lane = lax.broadcasted_iota(jnp.int32, (n, LANES), 1)
    parts, last = [], None
    for i in range(3):
        part = value[i * n : (i + 1) * n]
        parts.append(pltpu.roll(part, cut, 1))
        rest = pltpu.roll(part, (cut + i * side - PACKED) % LANES, 1)
        last = rest if i == 0 else jnp.where(lane >= cut + i * side, rest, last)
    return jnp.concatenate([*parts, last], axis=0)


def window_body(count, rows, tile_ref, strip_ref, *refs):
    outs, ext = refs[:count], refs[count]
    me = lax.axis_index("tm")
    wide = tile_ref.shape[1] // count
    extend(ext, 0, 2 * rows, tile_ref[: 2 * rows, :], strip_ref[: 2 * rows, :])
    for d in range(count):
        outs[d][...] = window(ext, 0, 2 * rows, wide * (me ^ d))


def edge_body(count, rows, tile_ref, strip_ref, after, *refs):
    del after
    outs, (coef_ref, down_ref, up_ref, ext) = refs[:count], refs[count:]
    me = lax.axis_index("tm")
    cols = tile_ref.shape[1]
    wide = cols // count
    extend(ext, 0, 9 * rows, tile_ref[2 * rows :, :], strip_ref[2 * rows :, :])
    coef_ref[...] = window(ext, 2 * rows, 9 * rows, wide * me)
    for d in range(count):
        outs[d][: 2 * rows * PACKED // LANES, :] = packed(
            window(ext, 0, 2 * rows, wide * (me ^ d))
        )
    at = edge_rows((down_ref, up_ref), coef_ref, 0, EARLY, 0)
    lane = lax.broadcasted_iota(jnp.int32, (SUB, LANES), 1)
    sides = [None, None]
    for sp in range(2):
        lo = (2 + sp) * rows
        starts = (lo + rows - HALO_W, lo)
        for i in range(cols // LANES):
            send_rows(
                (down_ref, up_ref),
                slice(at, at + HALO_W),
                *[tile_ref[p : p + HALO_W, i * LANES : (i + 1) * LANES] for p in starts],
            )
            at += HALO_W
        for i in range(HALO_W // SUB):
            n = sp * (HALO_W // SUB) + i
            for side, p in enumerate(starts):
                strip = strip_ref[p + i * SUB : p + (i + 1) * SUB, :]
                strip = jnp.where(
                    lax.axis_index("sy") == 0,
                    pltpu.roll(strip, n * SIDE, 1),
                    pltpu.roll(strip, (n + 1) * SIDE % LANES, 1),
                )
                sides[side] = (
                    strip if n == 0 else jnp.where(lane >= n * SIDE, strip, sides[side])
                )
    send_rows((down_ref, up_ref), slice(at, at + SUB), *sides)


def adjoint_window_body(count, rows, cols, top_ref, bot_ref, after, *refs):
    del after
    outs, ext = refs[count : 2 * count], refs[2 * count]
    me = lax.axis_index("tm")
    wide = cols // count
    for sp in range(2):
        base = sp * 2 * HALO_W
        at = sum(EARLY) + sp * (cols // LANES) * HALO_W
        side_at = sum(EARLY) + 2 * (cols // LANES) * HALO_W
        pieces = [
            received((top_ref, bot_ref), at + i * HALO_W, at + (i + 1) * HALO_W)
            for i in range(cols // LANES)
        ]
        both = received((top_ref, bot_ref), side_at, side_at + SUB)
        for side, start in enumerate((base, base + HALO_W)):
            parts = [piece[side] for piece in pieces]
            sides = both[side]
            strips = []
            for i in range(HALO_W // SUB):
                n = sp * (HALO_W // SUB) + i
                strips.append(
                    jnp.where(
                        lax.axis_index("sy") == 0,
                        pltpu.roll(sides, (LANES - n * SIDE) % LANES, 1),
                        pltpu.roll(sides, (2 * LANES - (n + 1) * SIDE) % LANES, 1),
                    )
                )
            extend(
                ext,
                start,
                start + HALO_W,
                jnp.concatenate(parts, axis=1),
                jnp.concatenate(strips, axis=0),
            )
    for d in range(count):
        outs[d][2 * rows * PACKED // LANES :, :] = packed(
            window(ext, 0, 4 * HALO_W, wide * (me ^ d))
        )


def interleave_body(count, *refs):
    cens, (coef_ref, mid, down_ref, up_ref) = refs[:count], refs[count:]
    edge_rows((down_ref, up_ref), coef_ref, len(EARLY), LATE, (count - 1) * 2 * HALO)
    rows = cens[0].shape[0] // 2
    me = lax.axis_index("tm")
    for d in range(count):
        slab = me ^ (-d % count)
        g, j = slab // PER_GROUP, slab % PER_GROUP
        for sp in range(2):
            mid[g, pl.ds(sp * PER_GROUP + j, rows, stride=SUB), :] = cens[d][
                sp * rows : (sp + 1) * rows, :
            ]

        @pl.when(slab < count - 1)
        def _(d=d, slab=slab):
            for sp in range(2):
                at = pl.multiple_of((slab * 2 + sp) * HALO, SUB)
                send_rows(
                    (down_ref, up_ref),
                    pl.ds(at, HALO),
                    cens[d][(sp + 1) * rows - HALO : (sp + 1) * rows, :],
                    cens[d][sp * rows : sp * rows + HALO, :],
                )


def blocks(lo, hi):
    return [(r, min(r + BLOCK, hi)) for r in range(lo, hi, BLOCK)]


def shift(value, by):
    n = value.shape[0] // SUB
    return pltpu.roll(value.reshape(n, SUB, LANES), by, 1).reshape(n * SUB, LANES)


def at_rows(ref, lo, hi):
    return ref[lo * SUB : hi * SUB, :]


def masked(flag, value):
    return jnp.where(flag, value, jnp.zeros_like(value))


def each_group(groups, fn):
    if groups == 1:
        fn(0)
    else:
        lax.fori_loop(0, groups, lambda g, c: (fn(g), c)[1], 0)


def through_groups(groups, fn, carry):
    if groups == 1:
        fn(0, carry)
    else:
        lax.fori_loop(0, groups, fn, carry)


def slab_of(a, b):
    return lax.broadcasted_iota(jnp.int32, ((b - a) * SUB, LANES), 0) % PER_GROUP


def step(src, dst, lo, hi, coefs, seen=None):
    cv, ce, cd, cx = coefs[:4]
    for a, b in blocks(lo, hi):
        n = (b - a) * SUB
        rows = at_rows(src, a - 1, b + 1)
        face = at_rows(cv, a, b + 1)
        u = rows[SUB : SUB + n]
        e = at_rows(ce, a, b)
        east = pltpu.roll(u, LANES - 1, 1)
        new = at_rows(cd, a, b) * u + face[:n] * rows[:n] + face[SUB:] * rows[2 * SUB :]
        if len(coefs) > 4:
            new = new + at_rows(coefs[4], a, b)
        new = new + (e * east + pltpu.roll(e * u, 1, 1))
        new = new + at_rows(cx, a, b) * shift(u, PER_GROUP)
        dst[a * SUB : b * SUB, :] = new
        if seen is not None:
            seen(a, b, rows[:n], u, east, new)


def sweep(groups, one, two, lo, hi, coefs):
    for n in range(STEPS):
        src, dst = (two, one) if n % 2 else (one, two)
        each_group(
            groups,
            lambda g, src=src, dst=dst, n=n: step(
                src.at[g], dst.at[g], lo + n // 2 * 2, hi - n // 2 * 2, coefs
            ),
        )


def coarse(gd, cx, value, a, b):
    return at_rows(gd, a, b) * value + (STEPS * at_rows(cx, a, b)) * shift(value, PER_GROUP)


def load(groups, refs, tile_rows, mid, top_ref, bot_ref):
    end = HALO + tile_rows
    for g in range(groups):
        for ref in refs:
            ref[g, HALO * SUB : end * SUB, :] = mid[g]
        for j in range(PER_GROUP):
            for sp in range(2):
                slab = min(g * PER_GROUP + j, groups * PER_GROUP - 2)
                at = (slab * 2 + sp) * HALO
                values = received((top_ref, bot_ref), at, at + HALO)
                for value, start in zip(values, (0, end)):
                    for ref in refs:
                        first = start * SUB + sp * PER_GROUP + j
                        ref[g, pl.ds(first, HALO, stride=SUB), :] = value


def spread(ref, sp, value):
    for j in range(PER_GROUP):
        ref[pl.ds(sp * PER_GROUP + j, value.shape[0], stride=SUB), :] = value


def coef_body(count, tile_rows, wide, coef_ref, top_ref, bot_ref, *rest):
    cv, ce, cd, gd, react_ref, flat = rest
    total = tile_rows + 2 * HALO
    k, rate = joined_rows(flat, coef_ref, (top_ref, bot_ref), 0, EARLY, 0)
    row = lax.broadcasted_iota(jnp.int32, (total, LANES), 0) + (
        lax.axis_index("sx") * tile_rows - HALO
    )
    col = lax.broadcasted_iota(jnp.int32, (total, LANES), 1) + (
        lax.axis_index("sy") * (wide * count) + lax.axis_index("tm") * wide - SIDE
    )
    all_rows = tile_rows * lax.axis_size("sx")
    all_cols = wide * count * lax.axis_size("sy")
    half = 0.5 * TIME_STEP
    above = half * (k + pltpu.roll(k, 1, 0))
    below = half * (k + pltpu.roll(k, total - 1, 0))
    east = half * (k + pltpu.roll(k, LANES - 1, 1))
    west = half * (k + pltpu.roll(k, 1, 1))
    faces = above + below + east + west
    above = jnp.where((row >= 1) & (row < all_rows), above, 0.0)
    east = jnp.where((col >= 0) & (col < all_cols - 1), east, 0.0)
    react = TIME_STEP * rate
    react_ref[...] = react
    for sp in range(2):
        spread(cv, sp, DIFFUSION[sp] * above)
        spread(ce, sp, DIFFUSION[sp] * east)
        spread(cd, sp, 1.0 - DIFFUSION[sp] * faces - DECAY[sp] * react)
        spread(gd, sp, 1.0 - (DECAY[sp] * STEPS) * react)


def state_body(
    count,
    tile_rows,
    mid,
    top_ref,
    bot_ref,
    coef_ref,
    cv,
    ce,
    cd,
    gd,
    react_ref,
    hist,
    slope,
    last_ref,
    cx,
    *rest,
):
    guess, one, two, cq, tg, flat = rest
    groups = count // PER_GROUP
    total = tile_rows + 2 * HALO
    coefs = (cv, ce, cd, cx, cq)
    coupling, *sources = joined_rows(
        flat, coef_ref, (top_ref, bot_ref), len(EARLY), LATE, (count - 1) * 2 * HALO
    )
    cross = react_ref[...] * coupling
    for sp in range(2):
        spread(cx, sp, cross)
        spread(cq, sp, TIME_STEP * sources[sp])
        spread(tg, sp, sources[2 + sp])
    lo, hi = STEPS, total - STEPS
    load(groups, (guess, one), tile_rows, mid, top_ref, bot_ref)
    sweep(groups, one, two, 1, total - 1, coefs)
    for a, b in blocks(lo, hi):
        slab = slab_of(a, b)

        def chain(g, carry, a=a, b=b, slab=slab):
            x = at_rows(one.at[g], a, b) - coarse(gd, cx, at_rows(guess.at[g], a, b), a, b)
            value = carry
            for _ in range(PER_GROUP - 1):
                value = jnp.where(
                    slab == 0, carry, shift(coarse(gd, cx, value, a, b) + x, 1)
                )
            two[g, a * SUB : b * SUB, :] = value
            return shift(coarse(gd, cx, value, a, b) + x, SUB - PER_GROUP + 1)

        through_groups(groups, chain, jnp.zeros(((b - a) * SUB, LANES), jnp.float32))

    for t in range(STEPS):
        src, dst = (one, two) if t % 2 else (two, one)

        def run(g, src=src, dst=dst, t=t):
            def seen(a, b, before, here, east, new):
                hist[t, g, (a - lo) * SUB : (b - lo) * SUB, :] = here
                p, q = max(a, HALO), min(b, HALO + tile_rows)
                if p < q:
                    rise = (east - here)[(p - a) * SUB : (q - a) * SUB]
                    slope[t, g, (p - HALO) * SUB : (q - HALO) * SUB, :] = rise

            step(src.at[g], dst.at[g], lo + t // 2 * 2, hi - t // 2 * 2, coefs, seen)

        each_group(groups, run)
    w_lo, w_hi = 2 * STEPS, total - 2 * STEPS
    last_ref[...] = at_rows(two.at[groups - 1], w_lo, w_hi) - at_rows(tg, w_lo, w_hi)


def lag_body(count, tile_rows, *refs):
    cens, (cv, ce, cd, cx, gd, lag, guess, one, two) = refs[:count], refs[count:]
    groups = count // PER_GROUP
    total = tile_rows + 2 * HALO
    me = lax.axis_index("tm")
    for d in range(count):
        slab = me ^ d
        g, j = slab // PER_GROUP, slab % PER_GROUP
        split = 2 * tile_rows * PACKED // LANES
        inner, outer = unpacked(cens[d][:split, :]), unpacked(cens[d][split:, :])
        for sp in range(2):
            edge = 2 * HALO_W * sp
            for start, value in (
                (HALO, inner[sp * tile_rows : (sp + 1) * tile_rows]),
                (HALO - HALO_W, outer[edge : edge + HALO_W]),
                (HALO + tile_rows, outer[edge + HALO_W : edge + 2 * HALO_W]),
            ):
                at = pl.ds(start * SUB + sp * PER_GROUP + j, value.shape[0], stride=SUB)
                guess[g, at, :] = value
                one[g, at, :] = value
    sweep(groups, one, two, STEPS + 1, total - STEPS - 1, (cv, ce, cd, cx))
    w_lo, w_hi = 2 * STEPS, total - 2 * STEPS

    def run(g):
        for a, b in blocks(w_lo, w_hi):
            lag[g, (a - w_lo) * SUB : (b - w_lo) * SUB, :] = at_rows(
                one.at[g], a, b
            ) - coarse(gd, cx, at_rows(guess.at[g], a, b), a, b)

    each_group(groups, run)


def adjoint_body(count, tile_rows, lag, hist, slope, last_ref, cv, ce, cd, cx, gd, *rest):
    outs = rest[:count]
    one, two, fv, fh = rest[count:]
    groups = count // PER_GROUP
    total = tile_rows + 2 * HALO
    end = HALO + tile_rows
    coefs = (cv, ce, cd, cx)
    lo = STEPS
    me = lax.axis_index("tm")
    w_lo, w_hi = 2 * STEPS, total - 2 * STEPS
    for a, b in blocks(w_lo, w_hi):
        slab = slab_of(a, b)

        def chain(turn, carry, a=a, b=b, slab=slab):
            g = groups - 1 - turn
            y = lag[g, (a - w_lo) * SUB : (b - w_lo) * SUB, :]
            top = jnp.where(slab == PER_GROUP - 1, carry, 0.0)
            value = top
            for _ in range(PER_GROUP - 1):
                value = jnp.where(
                    slab == PER_GROUP - 1,
                    top,
                    shift(coarse(gd, cx, value, a, b) + y, SUB - 1),
                )
            two[g, a * SUB : b * SUB, :] = value
            return shift(coarse(gd, cx, value, a, b) + y, PER_GROUP - 1)

        through_groups(groups, chain, at_rows(last_ref, a - w_lo, b - w_lo))

    def clear(g):
        for r in (w_lo - 1, w_hi):
            for ref in (one, two):
                ref[g, r * SUB : (r + 1) * SUB, :] = jnp.zeros((SUB, LANES), jnp.float32)

    each_group(groups, clear)

    lane = lax.broadcasted_iota(jnp.int32, (tile_rows, LANES), 1)
    left = lane < LANES // 2

    def paired(first, second):
        return jnp.where(
            left,
            pltpu.roll(first, LANES - SIDE, 1),
            pltpu.roll(second, LANES // 2 - SIDE, 1),
        )

    for d in range(count):
        slab = me ^ d
        g, j = slab // PER_GROUP, slab % PER_GROUP
        s_rows = [
            hist[0, g, pl.ds((HALO - lo) * SUB + sp * PER_GROUP + j, tile_rows, stride=SUB), :]
            for sp in range(2)
        ]
        w_rows = [
            two[g, pl.ds(HALO * SUB + sp * PER_GROUP + j, tile_rows, stride=SUB), :]
            for sp in range(2)
        ]
        outs[d][0:tile_rows, :] = paired(*s_rows)
        outs[d][tile_rows : 2 * tile_rows, :] = paired(*w_rows)

    fv[...] = jnp.zeros_like(fv)
    fh[...] = jnp.zeros_like(fh)

    def products(t, g, a, b, before, here, east):
        for ref, stop in ((fv, end + 1), (fh, end)):
            p, q = max(a, HALO), min(b, stop)
            if p >= q:
                continue
            at = slice((p - HALO) * SUB, (q - HALO) * SUB)
            part = slice((p - a) * SUB, (q - a) * SUB)
            if ref is fv:
                u = hist[t, g, (p - lo - 1) * SUB : (q - lo) * SUB, :]
                ref[at, :] += (u[SUB:] - u[:-SUB]) * (here[part] - before[part])
            else:
                ref[at, :] += slope[t, g, at, :] * (east[part] - here[part])

    def back_step(src, dst, t, g, cut):
        step(
            src.at[g],
            dst.at[g],
            w_lo + cut,
            w_hi - cut,
            coefs,
            lambda a, b, before, here, east, new: products(t, g, a, b, before, here, east),
        )

    for t in range(STEPS - 1, 0, -1):
        src, dst = (two, one) if t % 2 else (one, two)
        cut = (STEPS - 1 - t) // 2 * 2
        each_group(
            groups,
            lambda g, src=src, dst=dst, t=t, cut=cut: back_step(src, dst, t, g, cut),
        )

    def finish(g):
        for a, b in blocks(HALO, end + 1):
            rows = at_rows(one.at[g], a - 1, b)
            here = rows[SUB:]
            products(0, g, a, b, rows[:-SUB], here, pltpu.roll(here, LANES - 1, 1))

    each_group(groups, finish)

    size = tile_rows * SUB
    fh[...] = fv[0:size, :] + fv[SUB : size + SUB, :] + fh[...] + pltpu.roll(fh[...], 1, 1)
    summed = []
    for sp in range(2):
        parts = [
            fh[pl.ds(sp * PER_GROUP + j, tile_rows, stride=SUB), :] for j in range(PER_GROUP)
        ]
        summed.append((parts[0] + parts[1]) + (parts[2] + parts[3]))
    gradient = (-0.5 * TIME_STEP) * (DIFFUSION[0] * summed[0] + DIFFUSION[1] * summed[1])
    middle = tile_rows // 2
    fold = jnp.where(
        left[:middle],
        pltpu.roll(gradient[:middle], LANES - SIDE, 1),
        pltpu.roll(gradient[middle:], LANES // 2 - SIDE, 1),
    )
    for d in range(count):
        outs[d][2 * tile_rows :, :] = fold


def collect_body(count, wide, *refs):
    parts = refs[:count]
    s_ref, w_ref, g_ref, held = refs[count:]
    me = lax.axis_index("tm")
    for d in range(count):
        held[me ^ (-d % count)] = parts[d][...]
    rows = g_ref.shape[0]
    middle = rows // 2
    per = LANES // wide
    lane = lax.broadcasted_iota(jnp.int32, (rows, LANES), 1)

    def joined(lo, hi, start, v):
        value = None
        for i in range(per):
            t = v * per + i
            piece = held[t, lo:hi, :]
            turn = (i * wide - start) % LANES
            if turn:
                piece = pltpu.roll(piece, turn, 1)
            value = piece if i == 0 else jnp.where(lane[: hi - lo] >= i * wide, piece, value)
        return value

    for v in range(count // per):
        at = slice(v * LANES, (v + 1) * LANES)
        for sp in range(2):
            start = sp * (LANES // 2)
            s_ref[sp * rows : (sp + 1) * rows, at] = joined(0, rows, start, v)
            w_ref[sp * rows : (sp + 1) * rows, at] = joined(rows, 2 * rows, start, v)
            g_ref[sp * middle : (sp + 1) * middle, at] = joined(
                2 * rows, 2 * rows + middle, start, v
            )


def local(state_guess, adjoint_guess, diffusivity, decay_rate, coupling, control, target):
    rows, cols = diffusivity.shape
    count = lax.axis_size("tm")
    groups = count // PER_GROUP
    wide = cols // count
    total = rows + 2 * HALO
    fields = (
        state_guess.reshape(2 * rows, cols),
        adjoint_guess.reshape(2 * rows, cols),
        diffusivity,
        decay_rate,
        coupling,
        control.reshape(2 * rows, cols),
        target.reshape(2 * rows, cols),
    )

    def exchanged(parts, far_first=True):
        order = range(count - 1, 0, -1) if far_first else range(1, count)
        return [parts[0]] + [
            lax.ppermute(parts[d], "tm", [(i, i ^ d) for i in range(count)]) for d in order
        ]

    def turned(first, second):
        n = lax.axis_size("sx")
        return (
            lax.ppermute(first, "sx", [(i, i ^ 1) for i in range(n)]),
            lax.ppermute(second, "sx", [(i, (i + (1 if i % 2 else n - 1)) % n) for i in range(n)]),
        )

    fields = [pltpu.with_memory_space_constraint(f, pltpu.HBM) for f in fields]
    sems = [pltpu.SemaphoreType.DMA((7,))]
    (strip,) = call(strip_body, [(11 * rows, LANES)], sems, inputs=[HBM_SPEC] * 7)(*fields)
    (tile,) = call(tile_body, [(11 * rows, cols)], sems, inputs=[HBM_SPEC] * 7 + [VMEM_SPEC])(
        *fields, strip
    )
    strip = lax.ppermute(strip, "sy", [(0, 1), (1, 0)])
    edge = (sum(EARLY) + 2 * (cols // LANES) * HALO_W + SUB, LANES)
    windows = call(
        functools.partial(window_body, count, rows),
        [(2 * rows, LANES)] * count,
        [pltpu.VMEM((2 * rows, cols + 2 * LANES), jnp.float32)],
    )(tile, strip)
    states = exchanged(windows)
    size = 2 * (rows + 2 * HALO_W) * PACKED // LANES
    *inner, coef, down, up = call(
        functools.partial(edge_body, count, rows),
        [(size, LANES)] * count + [(7 * rows, LANES), edge, edge],
        [pltpu.VMEM((9 * rows, cols + 2 * LANES), jnp.float32)],
    )(tile, strip, windows[0])
    edges = turned(down, up)
    mid, down, up = call(
        functools.partial(interleave_body, count),
        [(groups, rows * SUB, LANES)] + [((count - 1) * 2 * HALO + sum(LATE), LANES)] * 2,
    )(*states, coef)
    state_edges = turned(down, up)
    windows = call(
        functools.partial(adjoint_window_body, count, rows, cols),
        [(size, LANES)] * count,
        [pltpu.VMEM((4 * HALO_W, cols + 2 * LANES), jnp.float32)],
        aliases={3 + d: d for d in range(count)},
    )(*edges, mid, *inner)
    adjoints = exchanged(windows, far_first=False)
    plain = (total * SUB, LANES)
    work = pltpu.VMEM((groups, total * SUB, LANES), jnp.float32)
    limit = 60 << 20 if groups > 1 else 32 << 20
    cv, ce, cd, gd, react = call(
        functools.partial(coef_body, count, rows, wide),
        [plain] * 4 + [(total, LANES)],
        [pltpu.VMEM((len(EARLY), total, LANES), jnp.float32)],
    )(coef, *edges)
    hist, slope, last, cx = call(
        functools.partial(state_body, count, rows),
        [
            (STEPS, groups, (total - 2 * STEPS) * SUB, LANES),
            (STEPS, groups, rows * SUB, LANES),
            ((total - 4 * STEPS) * SUB, LANES),
            plain,
        ],
        [
            *([work] * 3),
            *([pltpu.VMEM(plain, jnp.float32)] * 2),
            pltpu.VMEM((len(LATE), total, LANES), jnp.float32),
        ],
        limit,
    )(mid, *state_edges, coef, cv, ce, cd, gd, react)
    (lag,) = call(
        functools.partial(lag_body, count, rows),
        [(groups, (total - 4 * STEPS) * SUB, LANES)],
        [work] * 3,
        limit,
    )(*adjoints, cv, ce, cd, cx, gd)
    outs = call(
        functools.partial(adjoint_body, count, rows),
        [(2 * rows + rows // 2, LANES)] * count,
        [
            *([work] * 2),
            pltpu.VMEM(((rows + 1) * SUB, LANES), jnp.float32),
            pltpu.VMEM((rows * SUB, LANES), jnp.float32),
        ],
        limit,
    )(lag, hist, slope, last, cv, ce, cd, cx, gd)
    outs = exchanged(outs)
    states, adjoints, gradient = call(
        functools.partial(collect_body, count, wide),
        [(2 * rows, cols), (2 * rows, cols), (rows, cols)],
        [pltpu.VMEM((count, 2 * rows + rows // 2, LANES), jnp.float32)],
    )(*outs)
    return (
        states.reshape(1, 2, rows, cols),
        adjoints.reshape(1, 2, rows, cols),
        gradient,
    )


def solution(mesh):
    placed = (
        P("tm", None, "sx", "sy"),
        P("tm", None, "sx", "sy"),
        P("sx", "sy"),
        P("sx", "sy"),
        P("sx", "sy"),
        P(None, "sx", "sy"),
        P(None, "sx", "sy"),
    )
    return jax.shard_map(
        local,
        mesh=mesh,
        in_specs=placed,
        out_specs=(P("tm", None, "sx", "sy"), P("tm", None, "sx", "sy"), P("sx", "sy")),
        check_vma=False,
    )
```
